32 devices in a mesh: regroup: 2 (over y), loop: 4 (over z), replica: 4 (over x, core).
Axes of the slice: x: 2, y: 2, z: 4, core: 2. Of those that a mesh axis runs over, the one named last changes fastest.
Arguments:
- features: bfloat16 [4, 4, 1024, 256], P('replica', 'loop', None, 'regroup'), may hold values from -6 to 6
- weight: bfloat16 [256, 256], replicated, may hold values from -0.375 to 0.375
- tiles: bfloat16 [4, 4, 2, 32, 128, 128], P('replica', 'loop', 'regroup'), may hold values from 0 to 1, as said below
- tile_row: int32 [4, 4, 2, 32], P('replica', 'loop', 'regroup'), may hold values from 0 to 3, as said below
- tile_col: int32 [4, 4, 2, 32], P('replica', 'loop', 'regroup'), may hold values from 0 to 3, as said below
- tile_width: int32 [4, 4, 2, 32], P('replica', 'loop', 'regroup'), may hold values from 0 to 128, as said below
- cotangent: bfloat16 [4, 4, 2, 512, 256], P('replica', 'loop', 'regroup'), may hold values from -6 to 6
Outputs:
- output: bfloat16 [4, 4, 2, 512, 256], P('replica', 'loop', 'regroup')
- grad_feat: bfloat16 [4, 4, 1024, 256], P('replica', 'loop', None, 'regroup')
- grad_weight: float32 [256, 256], replicated
The draws below stay inside these ranges and needn't reach their ends.
Inputs may be any that keep to these rules, and one draw needn't show every extreme that they name: `tiles`: entries are 0 or between 0.25 and 1. `tile_row`: slot k < 4 of every device names cell block k. tile_col[r, l, g, s] is l - 1, l or l + 1 modulo 4. `tile_width`: each device's live slots come first, from 4 to 32 of them; some device has exactly 4 live and some all 32; slot 0 is live with width 128.
All inputs are finite; a program needn't handle non-finite values.
Results may differ from the reference program's by a relative error of at most 0.013.
Values may be sent and summed in bfloat16 or wider, within the bound.
A program may use at most 64 MiB of HBM per device.

```python
import math
import jax
import jax.numpy as jnp
from jax import lax

F = 256
TILE = 128
CELLS_DEV = 512
TILES = 32
RB = 4
NETS = 512
ROWS_LOOP = 1024
ALL_CELLS = 16384
N_REGROUP = 2
N_LOOP = 4
N_REPLICA = 4


def draw_tiles(key, part):
    shape = (N_REPLICA, N_LOOP, N_REGROUP, TILES, TILE, TILE)
    key_value, key_keep = jax.random.split(key)
    values = jax.random.uniform(key_value, shape, jnp.float32, 0.25, 1.0)
    spread = max(TILE * max(TILES // RB, 1) // 8, 2)
    keep = jax.random.randint(key_keep, shape, 0, spread) == 0
    return jnp.where(keep, values, jnp.float32(0.0)).astype(jnp.bfloat16)


def draw_tile_row(key, part):
    shape = (N_REPLICA, N_LOOP, N_REGROUP, TILES)
    random_rows = jax.random.randint(key, shape, 0, RB)
    slot = jnp.arange(TILES, dtype=jnp.int32)
    return jnp.where(slot < RB, slot, random_rows).astype(jnp.int32)


def draw_tile_col(key, part):
    shape = (N_REPLICA, N_LOOP, N_REGROUP, TILES)
    offset = jax.random.randint(key, shape, -1, 2)
    home = jnp.arange(N_LOOP, dtype=jnp.int32)[None, :, None, None]
    return ((home + offset + N_LOOP) % N_LOOP).astype(jnp.int32)


def draw_tile_width(key, part):
    shape = (N_REPLICA, N_LOOP, N_REGROUP, TILES)
    key_count, key_full, key_width = jax.random.split(key, 3)
    levels = jax.random.randint(key_count, shape[:3], 0, 4)
    counts = jnp.maximum(jnp.right_shift(jnp.int32(TILES), levels), RB).reshape(-1)
    total = N_REPLICA * N_LOOP * N_REGROUP
    chosen = jax.random.randint(key_full, (), 0, total)
    lowest = (chosen + 1) % total
    counts = counts.at[chosen].set(TILES).at[lowest].set(RB).reshape(shape[:3])
    slot = jnp.arange(TILES, dtype=jnp.int32)
    widths = jax.random.randint(key_width, shape, 1, TILE + 1)
    widths = jnp.where(slot == 0, TILE, widths)
    return jnp.where(slot < counts[..., None], widths, 0).astype(jnp.int32)


def shard_levels(stream_key, extent, shards, least, largest):
    def one(axis_at, parts):
        steps = jax.random.uniform(jax.random.fold_in(jax.random.fold_in(stream_key, 6), axis_at), (parts,), jnp.float32, least / len(shards), largest / len(shards))
        return jnp.repeat(jnp.exp(steps), extent[axis_at] // parts).reshape((-1,) + (1,) * (len(extent) - axis_at - 1))

    factor_of = one(*shards[0])
    for cut in shards[1:]:
        factor_of = factor_of * one(*cut)
    return factor_of


def bell_draw(rng, shape, scale, limit, pieces=(), held_as=jnp.bfloat16):
    values = jax.random.normal(rng, shape, jnp.float32) * scale
    if len(pieces) > 0:
        values = shard_levels(rng, shape, pieces, -0.22, 0.18) * values
    return jnp.clip(values, min=-limit, max=limit).astype(held_as)


def setup_inputs(seed: int = 0) -> dict:
    streams_of = jax.random.split(jax.random.key(seed), 8)
    return {
        "features": bell_draw(streams_of[0], (N_REPLICA, N_LOOP, ROWS_LOOP, F), 1.0, 6.0, ((0, 4), (1, 4), (3, 2))),
        "weight": bell_draw(streams_of[1], (F, F), F ** -0.5, 0.375),
        "tiles": draw_tiles(jax.random.fold_in(streams_of[7], 71), 0),
        "tile_row": draw_tile_row(jax.random.fold_in(streams_of[7], 71), 0),
        "tile_col": draw_tile_col(jax.random.fold_in(streams_of[7], 71), 0),
        "tile_width": draw_tile_width(jax.random.fold_in(streams_of[7], 71), 0),
        "cotangent": bell_draw(streams_of[6], (N_REPLICA, N_LOOP, N_REGROUP, CELLS_DEV, F), 1.0, 6.0, ((0, 4), (1, 4), (2, 2))),
    }


EPSILON = 1e-06
HIGH = lax.Precision.HIGHEST

def rms_scale(values):
    return values * lax.rsqrt(lax.optimization_barrier(jnp.mean(values * values, axis=-1, keepdims=True)) + EPSILON)

def region(cell_rows, live_raw, rows_idx, cols_idx, widths, grad_out, weight):
    column = jnp.arange(TILE, dtype=jnp.int32)
    live_tiles = jnp.where(column[None, None, None, :] < widths[:, :, None, None], live_raw, jnp.zeros((), live_raw.dtype)).astype(jnp.float32)
    row_hot = (rows_idx[:, :, None] == jnp.arange(RB, dtype=jnp.int32)[None, None, :]).astype(jnp.float32)
    col_hot = (cols_idx[:, :, None] == jnp.arange(N_LOOP, dtype=jnp.int32)[None, None, :]).astype(jnp.float32)
    row_sums = jnp.einsum('ltr,lti->lri', row_hot, lax.optimization_barrier(jnp.sum(live_tiles, axis=3)), precision=HIGH)
    cell_deg = 1.0 + row_sums.reshape(N_LOOP, CELLS_DEV)
    cell_root = jnp.sqrt(cell_deg)[:, :, None]
    col_part = jnp.einsum('ltc,ltj->lcj', col_hot, lax.optimization_barrier(jnp.sum(live_tiles, axis=2)), precision=HIGH).astype(jnp.bfloat16)
    net_deg = 1.0 + lax.optimization_barrier(jnp.sum(col_part.astype(jnp.float32), axis=0)).reshape(NETS)

    def to_nets(values):
        blocked = values.reshape(N_LOOP, RB, TILE, F).astype(jnp.float32)
        gathered = jnp.take_along_axis(blocked, rows_idx[:, :, None, None], axis=1)
        per_tile = jnp.einsum('ltij,ltif->ltjf', live_tiles, gathered, precision=HIGH)
        partial_value = jnp.einsum('ltc,ltjf->lcjf', col_hot, per_tile, precision=HIGH).astype(jnp.bfloat16)
        return lax.optimization_barrier(jnp.sum(partial_value.astype(jnp.float32), axis=0)).reshape(NETS, F)

    def from_nets(values):
        gathered = values.reshape(N_LOOP, TILE, F).astype(jnp.float32)[cols_idx]
        per_tile = jnp.einsum('ltij,ltjf->ltif', live_tiles, gathered, precision=HIGH)
        return jnp.einsum('ltr,ltif->lrif', row_hot, per_tile, precision=HIGH).reshape(N_LOOP, CELLS_DEV, F)
    mixed = jnp.einsum('lcf,fg->lcg', cell_rows.astype(jnp.float32), weight.astype(jnp.float32), precision=HIGH).astype(jnp.bfloat16)
    scaled = (mixed.astype(jnp.float32) / cell_root).astype(jnp.bfloat16)
    net_feat = (to_nets(scaled) / net_deg[:, None]).astype(jnp.bfloat16)
    gathered_z = from_nets(net_feat) / cell_root
    normed, norm_back = jax.vjp(rms_scale, gathered_z)
    before = mixed.astype(jnp.float32) + normed
    output = jax.nn.silu(before).astype(jnp.bfloat16)
    sigmoid_v = jax.nn.sigmoid(before)
    grad_before = grad_out.astype(jnp.float32) * sigmoid_v * (1.0 + before * (1.0 - sigmoid_v))
    grad_z = norm_back(grad_before)[0]
    grad_scaled = (grad_z / cell_root).astype(jnp.bfloat16)
    grad_net = (to_nets(grad_scaled) / net_deg[:, None]).astype(jnp.bfloat16)
    grad_mixed = (grad_before + from_nets(grad_net) / cell_root).astype(jnp.bfloat16)
    grad_rows = jnp.einsum('lcg,fg->lcf', grad_mixed.astype(jnp.float32), weight.astype(jnp.float32), precision=HIGH).astype(jnp.bfloat16)
    weight_term = jnp.einsum('lcf,lcg->fg', cell_rows.astype(jnp.float32), grad_mixed.astype(jnp.float32), precision=HIGH)
    return (output, grad_rows, weight_term)

def reference(features, weight, tiles, tile_row, tile_col, tile_width, cotangent):
    groups = N_REPLICA * N_REGROUP
    cell_rows = features.reshape(N_REPLICA, N_LOOP, N_REGROUP, CELLS_DEV, F).transpose(0, 2, 1, 3, 4).reshape(groups, N_LOOP, CELLS_DEV, F)
    tile_sets = tiles.transpose(0, 2, 1, 3, 4, 5).reshape(groups, N_LOOP, TILES, TILE, TILE)
    rows_idx = tile_row.transpose(0, 2, 1, 3).reshape(groups, N_LOOP, TILES)
    cols_idx = tile_col.transpose(0, 2, 1, 3).reshape(groups, N_LOOP, TILES)
    widths = tile_width.transpose(0, 2, 1, 3).reshape(groups, N_LOOP, TILES)
    grad_out = cotangent.transpose(0, 2, 1, 3, 4).reshape(groups, N_LOOP, CELLS_DEV, F)

    def one(items):
        return region(items[0], items[1], items[2], items[3], items[4], items[5], weight)
    outs = lax.map(one, (cell_rows, tile_sets, rows_idx, cols_idx, widths, grad_out))
    output = outs[0].reshape(N_REPLICA, N_REGROUP, N_LOOP, CELLS_DEV, F).transpose(0, 2, 1, 3, 4)
    grad_feat = outs[1].reshape(N_REPLICA, N_REGROUP, N_LOOP, CELLS_DEV, F).transpose(0, 2, 1, 3, 4).reshape(N_REPLICA, N_LOOP, N_REGROUP * CELLS_DEV, F)
    grad_weight = lax.optimization_barrier(jnp.sum(outs[2], axis=0)) * (1.0 / math.sqrt(ALL_CELLS))
    return (output, grad_feat, grad_weight)
```

```python
import functools
import math

import jax
import jax.numpy as jnp
from jax import lax
from jax.experimental import pallas as pl
from jax.experimental.pallas import tpu as pltpu
from jax.sharding import PartitionSpec as P

EPSILON = 1e-06
MESH = pl.DeviceIdType.MESH
F32 = jnp.float32
BF16 = jnp.bfloat16


def mm(a, b):
    return jnp.dot(a, b, preferred_element_type=F32)


def mm_nt(a, b):
    return lax.dot_general(a, b, (((1,), (1,)), ((), ())), preferred_element_type=F32)


def layer_kernel(
    groups, loops, replicas,
    row_ref, col_ref, width_ref, feat_hbm, weight_ref, tiles_hbm, cot_hbm,
    out_hbm, gf_hbm, gw_ref,
    tiles_ref, cot_ref, x_ref, xt_ref, h_ref, ht_ref, rs_ref, y_ref, q_ref, acc_ref, dpre_ref,
    out_ref, gf_ref, deg_s, deg_r, deinv_ref, part_s, part_r, net_ref, gpart_s, gpart_r, gnet_ref,
    wg_s, wg_r, wz_ref, wf_ref,
    local_sem, feat_ss, feat_rs, deg_ss, deg_rs, part_ss, part_rs, net_ss, net_rs,
    gpart_ss, gpart_rs, gnet_ss, gnet_rs, gf_ss, gf_rs, wg_ss, wg_rs, wz_ss, wz_rs, wf_ss, wf_rs,
):
    slots, edge, _ = tiles_hbm.shape
    cells, chans = cot_hbm.shape
    fw = feat_hbm.shape[1]
    plane = groups * replicas
    my_g = lax.axis_index("regroup")
    my_l = lax.axis_index("loop")
    my_r = lax.axis_index("replica")
    my_p = my_r * groups + my_g

    def group_peer(k):
        return lax.rem(my_g + k, groups)

    def loop_peer(k):
        return lax.rem(my_l + k, loops)

    def plane_peer(k):
        peer = lax.rem(my_p + k, plane)
        return peer, {"replica": lax.div(peer, groups), "regroup": lax.rem(peer, groups)}

    prev_dev = {"loop": loop_peer(loops - 1)}
    next_dev = {"loop": loop_peer(1)}

    def remote(src, dst, ss, rs, dev):
        return pltpu.make_async_remote_copy(
            src_ref=src, dst_ref=dst, send_sem=ss, recv_sem=rs, device_id=dev,
            device_id_type=MESH)

    barrier = pltpu.get_barrier_semaphore()
    for k in range(1, plane):
        pl.semaphore_signal(barrier, inc=1, device_id=plane_peer(k)[1], device_id_type=MESH)
    for k in range(1, loops):
        pl.semaphore_signal(barrier, inc=1, device_id={"loop": loop_peer(k)}, device_id_type=MESH)

    tiles_copy = pltpu.make_async_copy(tiles_hbm, tiles_ref, local_sem.at[0])
    tiles_copy.start()
    own_rows = pl.ds(pl.multiple_of(my_g * cells, cells), cells)
    own_copy = pltpu.make_async_copy(feat_hbm.at[own_rows], x_ref.at[my_g], local_sem.at[1])
    own_copy.start()
    cot_copy = pltpu.make_async_copy(cot_hbm, cot_ref, local_sem.at[2])
    cot_copy.start()

    pl.semaphore_wait(barrier, plane - 1 + loops - 1)

    feat_copies = []
    for k in range(1, groups):
        peer = group_peer(k)
        rows = pl.ds(pl.multiple_of(peer * cells, cells), cells)
        copy = remote(feat_hbm.at[rows], x_ref.at[my_g], feat_ss.at[k], feat_rs.at[k],
                      {"regroup": peer})
        copy.start()
        feat_copies.append(copy)

    tiles_copy.wait()
    half = edge // 2
    lane = lax.broadcasted_iota(jnp.int32, (1, edge), 1)

    def build(rh, carry):
        block = lax.div(rh, 2)
        base = pl.multiple_of(lax.rem(rh, 2) * half, half)

        def add_tile(t, sums):
            tile = tiles_ref[t, pl.ds(base, half), :].astype(F32)
            place = lax.rem(col_ref[t] - my_l + loops, loops)
            live = jnp.where(row_ref[t] == block, width_ref[t], 0)
            spot = jnp.where(place == 0, 1, jnp.where(place == 1, 2, 0))
            new = []
            for c in range(3):
                mask = (lane < jnp.where(spot == c, live, 0)).astype(F32)
                new.append(sums[c] + tile * mask)
            return tuple(new)

        zero = jnp.zeros((half, edge), F32)
        sums = lax.fori_loop(0, slots, add_tile, (zero, zero, zero), unroll=4)
        rows = pl.ds(pl.multiple_of(rh * half, half), half)
        for c in range(3):
            h_ref[rows, c * edge:(c + 1) * edge] = sums[c].astype(BF16)
        return carry

    lax.fori_loop(0, cells // half, build, 0)
    for c in range(3):
        ht_ref[c * edge:(c + 1) * edge, :] = h_ref[:, c * edge:(c + 1) * edge].T

    deg_s[...] = mm(ht_ref[...], jnp.ones((cells, edge), BF16)).astype(BF16).reshape(3, edge, edge)
    deg_copies = [
        remote(deg_s.at[0], deg_r.at[1], deg_ss.at[0], deg_rs.at[1], prev_dev),
        remote(deg_s.at[2], deg_r.at[0], deg_ss.at[1], deg_rs.at[0], next_dev),
    ]
    for copy in deg_copies:
        copy.start()
    rs_ref[...] = lax.rsqrt(1.0 + mm(h_ref[...], jnp.ones((3 * edge, chans), BF16)))

    own_copy.wait()
    for copy in feat_copies:
        copy.wait_recv()
    y32 = mm(x_ref[0], weight_ref[0:fw, :])
    for g in range(1, groups):
        y32 = y32 + mm(x_ref[g], weight_ref[g * fw:(g + 1) * fw, :])
    y16 = y32.astype(BF16)
    y_ref[...] = y16
    q_ref[...] = (y16.astype(F32) * rs_ref[...]).astype(BF16)

    def exchange_sums(send_buf, recv_buf, ss, rs):
        send_buf[0] = mm(ht_ref[0:edge, :], q_ref[...]).astype(BF16)
        down = remote(send_buf.at[0], recv_buf.at[1], ss.at[0], rs.at[1], prev_dev)
        down.start()
        send_buf[1] = mm(ht_ref[2 * edge:, :], q_ref[...]).astype(BF16)
        up = remote(send_buf.at[1], recv_buf.at[0], ss.at[1], rs.at[0], next_dev)
        up.start()
        own = mm(ht_ref[edge:2 * edge, :], q_ref[...]).astype(BF16).astype(F32)
        return own, (down, up)

    def exchange_nets(own, recv_buf, net, ss, rs):
        total = own + recv_buf[0].astype(F32) + recv_buf[1].astype(F32)
        net[1] = (total * deinv_ref[...]).astype(BF16)
        down = remote(net.at[1], net.at[2], ss.at[0], rs.at[1], prev_dev)
        up = remote(net.at[1], net.at[0], ss.at[1], rs.at[0], next_dev)
        down.start()
        up.start()
        acc_ref[...] = mm(h_ref[:, edge:2 * edge], net[1])
        return (down, up)

    own, part_copies = exchange_sums(part_s, part_r, part_ss, part_rs)
    for g in range(groups):
        xt_ref[g * fw:(g + 1) * fw, :] = x_ref[g].T
    for copy in deg_copies:
        copy.wait_recv()
    degree = (1.0 + deg_s[1].astype(F32) + deg_r[0].astype(F32) + deg_r[1].astype(F32))
    inverse = 1.0 / degree
    for c in range(chans // edge):
        deinv_ref[:, c * edge:(c + 1) * edge] = inverse
    for copy in part_copies:
        copy.wait_recv()
    net_copies = exchange_nets(own, part_r, net_ref, net_ss, net_rs)
    cot_copy.wait()
    for copy in net_copies:
        copy.wait_recv()
    acc_ref[...] += mm(h_ref[:, 0:edge], net_ref[0]) + mm(h_ref[:, 2 * edge:], net_ref[2])

    step = 64

    def middle(i, carry):
        rows = pl.ds(pl.multiple_of(i * step, step), step)
        root = rs_ref[rows, :]
        z = acc_ref[rows, :] * root
        inv = lax.rsqrt(jnp.mean(z * z, axis=-1, keepdims=True) + EPSILON)
        normed = z * inv
        pre = y_ref[rows, :].astype(F32) + normed
        sig = 1.0 / (1.0 + jnp.exp(-pre))
        out_ref[rows, :] = (pre * sig).astype(BF16)
        dpre = cot_ref[rows, :].astype(F32) * sig * (1.0 + pre * (1.0 - sig))
        dpre_ref[rows, :] = dpre
        dz = inv * (dpre - normed * jnp.mean(dpre * normed, axis=-1, keepdims=True))
        q_ref[rows, :] = (dz * root).astype(BF16)
        return carry

    lax.fori_loop(0, cells // step, middle, 0)
    out_copy = pltpu.make_async_copy(out_ref, out_hbm, local_sem.at[3])

    own, gpart_copies = exchange_sums(gpart_s, gpart_r, gpart_ss, gpart_rs)
    out_copy.start()
    for copy in gpart_copies:
        copy.wait_recv()
    gnet_copies = exchange_nets(own, gpart_r, gnet_ref, gnet_ss, gnet_rs)
    for copy in gnet_copies:
        copy.wait_recv()
    acc_ref[...] += mm(h_ref[:, 0:edge], gnet_ref[0]) + mm(h_ref[:, 2 * edge:], gnet_ref[2])
    dy = (dpre_ref[...] + acc_ref[...] * rs_ref[...]).astype(BF16)
    q_ref_dy = y_ref
    q_ref_dy[...] = dy

    rows_p = chans // plane
    wg = mm(xt_ref[...], q_ref_dy[...])
    for p in range(plane):
        wg_s[p] = wg[p * rows_p:(p + 1) * rows_p].astype(wg_s.dtype)
    wg_copies = []
    for k in range(1, plane):
        peer, dev = plane_peer(k)
        copy = remote(wg_s.at[peer], wg_r.at[my_p], wg_ss.at[k], wg_rs.at[k], dev)
        copy.start()
        wg_copies.append(copy)
    wg_r[my_p] = wg_s[my_p]

    gf_copies = []
    for k in range(1, groups):
        peer = group_peer(k)
        w_rows = weight_ref[pl.ds(pl.multiple_of(peer * fw, fw), fw), :]
        gf_ref[k] = mm_nt(q_ref_dy[...], w_rows).astype(BF16)
        copy = remote(gf_ref.at[k], gf_hbm.at[own_rows], gf_ss.at[k], gf_rs.at[k],
                      {"regroup": peer})
        copy.start()
        gf_copies.append(copy)
    w_rows = weight_ref[pl.ds(pl.multiple_of(my_g * fw, fw), fw), :]
    gf_ref[0] = mm_nt(q_ref_dy[...], w_rows).astype(BF16)
    gf_own = pltpu.make_async_copy(gf_ref.at[0], gf_hbm.at[own_rows], local_sem.at[4])
    gf_own.start()

    for copy in wg_copies:
        copy.wait_recv()
    piece = wg_r[0].astype(F32)
    for p in range(1, plane):
        piece = piece + wg_r[p].astype(F32)
    wz_ref[my_l] = piece.astype(wz_ref.dtype)
    wz_copies = []
    for k in range(1, loops):
        copy = remote(wz_ref.at[my_l], wz_ref.at[my_l], wz_ss.at[k], wz_rs.at[k],
                      {"loop": loop_peer(k)})
        copy.start()
        wz_copies.append(copy)
    for copy in wz_copies:
        copy.wait_recv()
    piece = wz_ref[0].astype(F32)
    for l in range(1, loops):
        piece = piece + wz_ref[l].astype(F32)
    wf_ref[my_p] = piece.astype(wf_ref.dtype)
    wf_copies = []
    for k in range(1, plane):
        copy = remote(wf_ref.at[my_p], wf_ref.at[my_p], wf_ss.at[k], wf_rs.at[k],
                      plane_peer(k)[1])
        copy.start()
        wf_copies.append(copy)
    for copy in wf_copies:
        copy.wait_recv()
    scale = 1.0 / math.sqrt(cells * plane * loops)
    for p in range(plane):
        gw_ref[p * rows_p:(p + 1) * rows_p, :] = wf_ref[p].astype(F32) * scale

    for copy in gf_copies:
        copy.wait_recv()
    gf_own.wait()
    out_copy.wait()
    for copies in (feat_copies, deg_copies, part_copies, net_copies, gpart_copies, gnet_copies,
                   wg_copies, gf_copies, wz_copies, wf_copies):
        for copy in copies:
            copy.wait_send()


def per_device(groups, loops, replicas,
               features, weight, tiles, tile_row, tile_col, tile_width, cotangent):
    cells, chans = cotangent.shape[-2:]
    slots, edge = tiles.shape[-3:-1]
    total_rows, fw = features.shape[-2:]
    plane = groups * replicas
    rows_p = chans // plane
    link = BF16 if rows_p % 16 == 0 else F32
    smem = pl.BlockSpec(memory_space=pltpu.SMEM)
    vmem = pl.BlockSpec(memory_space=pltpu.VMEM)
    anym = pl.BlockSpec(memory_space=pl.ANY)
    dma = pltpu.SemaphoreType.DMA
    V = pltpu.VMEM
    scratch = [
        V((slots, edge, edge), BF16), V((cells, chans), BF16), V((groups, cells, fw), BF16),
        V((chans, cells), BF16), V((cells, 3 * edge), BF16), V((3 * edge, cells), BF16),
        V((cells, chans), F32), V((cells, chans), BF16), V((cells, chans), BF16),
        V((cells, chans), F32), V((cells, chans), F32), V((cells, chans), BF16),
        V((groups, cells, fw), BF16),
        V((3, edge, edge), BF16), V((2, edge, edge), BF16), V((edge, chans), F32),
        V((2, edge, chans), BF16), V((2, edge, chans), BF16), V((3, edge, chans), BF16),
        V((2, edge, chans), BF16), V((2, edge, chans), BF16), V((3, edge, chans), BF16),
        V((plane, rows_p, chans), link), V((plane, rows_p, chans), link),
        V((loops, rows_p, chans), link), V((plane, rows_p, chans), link),
        dma((5,)), dma((groups,)), dma((groups,)),
        dma((2,)), dma((2,)), dma((2,)), dma((2,)), dma((2,)), dma((2,)),
        dma((2,)), dma((2,)), dma((2,)), dma((2,)), dma((groups,)), dma((groups,)),
        dma((plane,)), dma((plane,)), dma((loops,)), dma((loops,)), dma((plane,)), dma((plane,)),
    ]
    out, gf, gw = pl.pallas_call(
        functools.partial(layer_kernel, groups, loops, replicas),
        out_shape=(
            jax.ShapeDtypeStruct((cells, chans), BF16),
            jax.ShapeDtypeStruct((total_rows, fw), BF16),
            jax.ShapeDtypeStruct((chans, chans), F32),
        ),
        in_specs=[smem, smem, smem, anym, vmem, anym, anym],
        out_specs=(anym, anym, vmem),
        scratch_shapes=scratch,
        compiler_params=pltpu.CompilerParams(
            collective_id=0, has_side_effects=True, vmem_limit_bytes=40 << 20),
    )(tile_row[0, 0, 0], tile_col[0, 0, 0], tile_width[0, 0, 0], features[0, 0], weight,
      tiles[0, 0, 0], cotangent[0, 0, 0])
    return out[None, None, None], gf[None, None], gw


def solution(mesh):
    sizes = dict(mesh.shape)
    return jax.shard_map(
        functools.partial(per_device, sizes["regroup"], sizes["loop"], sizes["replica"]),
        mesh=mesh,
        in_specs=(
            P("replica", "loop", None, "regroup"),
            P(),
            P("replica", "loop", "regroup", None, None, None),
            P("replica", "loop", "regroup", None),
            P("replica", "loop", "regroup", None),
            P("replica", "loop", "regroup", None),
            P("replica", "loop", "regroup", None, None),
        ),
        out_specs=(
            P("replica", "loop", "regroup", None, None),
            P("replica", "loop", None, "regroup"),
            P(),
        ),
        check_vma=False,
    )
```

```python
import functools
import math

import jax
import jax.numpy as jnp
from jax import lax
from jax.experimental import pallas as pl
from jax.experimental.pallas import tpu as pltpu
from jax.sharding import PartitionSpec as P

EPSILON = 1e-06
MESH = pl.DeviceIdType.MESH
F32 = jnp.float32
BF16 = jnp.bfloat16


def mm(a, b):
    return jnp.dot(a, b, preferred_element_type=F32)


def mm_nt(a, b):
    return lax.dot_general(a, b, (((1,), (1,)), ((), ())), preferred_element_type=F32)


def layer_kernel(
    groups, loops, replicas,
    row_hbm, col_hbm, width_hbm, feat_hbm, weight_hbm, tiles_hbm, cot_hbm,
    out_hbm, gf_out, wf_out,
    row_ref, col_ref, width_ref, weight_ref, tiles_ref, cot_ref, x_ref, xt_ref, h_ref, ht_ref, rs_ref, y_ref, q_ref, acc_ref, dpre_ref,
    out_ref, gf_ref, deg_s, deg_r, deinv_ref, part_s, part_r, net_ref, gpart_s, gpart_r, gnet_ref,
    wg_s, wg_r, wz_ref, wf_ref,
    local_sem, feat_ss, feat_rs, deg_ss, deg_rs, part_ss, part_rs, net_ss, net_rs,
    gpart_ss, gpart_rs, gnet_ss, gnet_rs, gf_ss, gf_rs, wg_ss, wg_rs, wz_ss, wz_rs, wf_ss, wf_rs,
):
    slots, edge, _ = tiles_hbm.shape
    cells, chans = cot_hbm.shape
    fw = feat_hbm.shape[1]
    plane = groups * replicas
    my_g = lax.axis_index("regroup")
    my_l = lax.axis_index("loop")
    my_r = lax.axis_index("replica")
    my_p = my_r * groups + my_g

    def group_peer(k):
        return lax.rem(my_g + k, groups)

    def loop_peer(k):
        return lax.rem(my_l + k, loops)

    def plane_peer(k):
        peer = lax.rem(my_p + k, plane)
        return peer, {"replica": lax.div(peer, groups), "regroup": lax.rem(peer, groups)}

    prev_dev = {"loop": loop_peer(loops - 1)}
    next_dev = {"loop": loop_peer(1)}

    def remote(src, dst, ss, rs, dev):
        return pltpu.make_async_remote_copy(
            src_ref=src, dst_ref=dst, send_sem=ss, recv_sem=rs, device_id=dev,
            device_id_type=MESH)

    barrier = pltpu.get_barrier_semaphore()
    for k in range(1, plane):
        pl.semaphore_signal(barrier, inc=1, device_id=plane_peer(k)[1], device_id_type=MESH)
    for k in range(1, loops):
        pl.semaphore_signal(barrier, inc=1, device_id={"loop": loop_peer(k)}, device_id_type=MESH)

    index_copies = [
        pltpu.make_async_copy(src, dst, local_sem.at[5 + i])
        for i, (src, dst) in enumerate(
            ((row_hbm, row_ref), (col_hbm, col_ref), (width_hbm, width_ref)))
    ]
    for copy in index_copies:
        copy.start()
    weight_copy = pltpu.make_async_copy(weight_hbm, weight_ref, local_sem.at[3])
    weight_copy.start()
    tiles_copy = pltpu.make_async_copy(tiles_hbm, tiles_ref, local_sem.at[0])
    tiles_copy.start()
    own_rows = pl.ds(pl.multiple_of(my_g * cells, cells), cells)
    own_copy = pltpu.make_async_copy(feat_hbm.at[own_rows], x_ref.at[my_g], local_sem.at[1])
    own_copy.start()
    cot_copy = pltpu.make_async_copy(cot_hbm, cot_ref, local_sem.at[2])
    cot_copy.start()

    pl.semaphore_wait(barrier, plane - 1 + loops - 1)

    feat_copies = []
    for k in range(1, groups):
        peer = group_peer(k)
        rows = pl.ds(pl.multiple_of(peer * cells, cells), cells)
        copy = remote(feat_hbm.at[rows], x_ref.at[my_g], feat_ss.at[k], feat_rs.at[k],
                      {"regroup": peer})
        copy.start()
        feat_copies.append(copy)

    for copy in index_copies:
        copy.wait()
    tiles_copy.wait()
    half = edge // 2
    lane = lax.broadcasted_iota(jnp.int32, (1, edge), 1)

    def build(rh, carry):
        block = lax.div(rh, 2)
        base = pl.multiple_of(lax.rem(rh, 2) * half, half)

        def add_tile(t, sums):
            tile = tiles_ref[t, pl.ds(base, half), :].astype(F32)
            place = lax.rem(col_ref[t] - my_l + loops, loops)
            live = jnp.where(row_ref[t] == block, width_ref[t], 0)
            spot = jnp.where(place == 0, 1, jnp.where(place == 1, 2, 0))
            new = []
            for c in range(3):
                mask = (lane < jnp.where(spot == c, live, 0)).astype(F32)
                new.append(sums[c] + tile * mask)
            return tuple(new)

        zero = jnp.zeros((half, edge), F32)
        sums = lax.fori_loop(0, slots, add_tile, (zero, zero, zero), unroll=4)
        rows = pl.ds(pl.multiple_of(rh * half, half), half)
        for c in range(3):
            h_ref[rows, c * edge:(c + 1) * edge] = sums[c].astype(BF16)
        return carry

    lax.fori_loop(0, cells // half, build, 0)
    for c in range(3):
        ht_ref[c * edge:(c + 1) * edge, :] = h_ref[:, c * edge:(c + 1) * edge].T

    deg_s[...] = mm(ht_ref[...], jnp.ones((cells, edge), BF16)).astype(BF16).reshape(3, edge, edge)
    deg_copies = [
        remote(deg_s.at[0], deg_r.at[1], deg_ss.at[0], deg_rs.at[1], prev_dev),
        remote(deg_s.at[2], deg_r.at[0], deg_ss.at[1], deg_rs.at[0], next_dev),
    ]
    for copy in deg_copies:
        copy.start()
    rs_ref[...] = lax.rsqrt(1.0 + mm(h_ref[...], jnp.ones((3 * edge, chans), BF16)))

    own_copy.wait()
    weight_copy.wait()
    for copy in feat_copies:
        copy.wait_recv()
    y32 = mm(x_ref[0], weight_ref[0:fw, :])
    for g in range(1, groups):
        y32 = y32 + mm(x_ref[g], weight_ref[g * fw:(g + 1) * fw, :])
    y16 = y32.astype(BF16)
    y_ref[...] = y16
    q_ref[...] = (y16.astype(F32) * rs_ref[...]).astype(BF16)

    def exchange_sums(send_buf, recv_buf, ss, rs):
        send_buf[0] = mm(ht_ref[0:edge, :], q_ref[...]).astype(BF16)
        down = remote(send_buf.at[0], recv_buf.at[1], ss.at[0], rs.at[1], prev_dev)
        down.start()
        send_buf[1] = mm(ht_ref[2 * edge:, :], q_ref[...]).astype(BF16)
        up = remote(send_buf.at[1], recv_buf.at[0], ss.at[1], rs.at[0], next_dev)
        up.start()
        own = mm(ht_ref[edge:2 * edge, :], q_ref[...]).astype(BF16).astype(F32)
        return own, (down, up)

    def exchange_nets(own, recv_buf, net, ss, rs):
        total = own + recv_buf[0].astype(F32) + recv_buf[1].astype(F32)
        net[1] = (total * deinv_ref[...]).astype(BF16)
        down = remote(net.at[1], net.at[2], ss.at[0], rs.at[1], prev_dev)
        up = remote(net.at[1], net.at[0], ss.at[1], rs.at[0], next_dev)
        down.start()
        up.start()
        acc_ref[...] = mm(h_ref[:, edge:2 * edge], net[1])
        return (down, up)

    own, part_copies = exchange_sums(part_s, part_r, part_ss, part_rs)
    for g in range(groups):
        xt_ref[g * fw:(g + 1) * fw, :] = x_ref[g].T
    for copy in deg_copies:
        copy.wait_recv()
    degree = (1.0 + deg_s[1].astype(F32) + deg_r[0].astype(F32) + deg_r[1].astype(F32))
    inverse = 1.0 / degree
    for c in range(chans // edge):
        deinv_ref[:, c * edge:(c + 1) * edge] = inverse
    for copy in part_copies:
        copy.wait_recv()
    net_copies = exchange_nets(own, part_r, net_ref, net_ss, net_rs)
    cot_copy.wait()
    for copy in net_copies:
        copy.wait_recv()
    acc_ref[...] += mm(h_ref[:, 0:edge], net_ref[0]) + mm(h_ref[:, 2 * edge:], net_ref[2])

    step = 64

    def middle(i, carry):
        rows = pl.ds(pl.multiple_of(i * step, step), step)
        root = rs_ref[rows, :]
        z = acc_ref[rows, :] * root
        inv = lax.rsqrt(jnp.mean(z * z, axis=-1, keepdims=True) + EPSILON)
        normed = z * inv
        pre = y_ref[rows, :].astype(F32) + normed
        sig = 1.0 / (1.0 + jnp.exp(-pre))
        out_ref[rows, :] = (pre * sig).astype(BF16)
        dpre = cot_ref[rows, :].astype(F32) * sig * (1.0 + pre * (1.0 - sig))
        dpre_ref[rows, :] = dpre
        dz = inv * (dpre - normed * jnp.mean(dpre * normed, axis=-1, keepdims=True))
        q_ref[rows, :] = (dz * root).astype(BF16)
        return carry

    lax.fori_loop(0, cells // step, middle, 0)
    out_copy = pltpu.make_async_copy(out_ref, out_hbm, local_sem.at[4])

    own, gpart_copies = exchange_sums(gpart_s, gpart_r, gpart_ss, gpart_rs)
    out_copy.start()
    for copy in gpart_copies:
        copy.wait_recv()
    gnet_copies = exchange_nets(own, gpart_r, gnet_ref, gnet_ss, gnet_rs)
    for copy in gnet_copies:
        copy.wait_recv()
    acc_ref[...] += mm(h_ref[:, 0:edge], gnet_ref[0]) + mm(h_ref[:, 2 * edge:], gnet_ref[2])
    dy = (dpre_ref[...] + acc_ref[...] * rs_ref[...]).astype(BF16)
    q_ref_dy = y_ref
    q_ref_dy[...] = dy

    rows_p = chans // plane
    wg = mm(xt_ref[...], q_ref_dy[...])
    for p in range(plane):
        wg_s[p] = wg[p * rows_p:(p + 1) * rows_p].astype(wg_s.dtype)
    wg_copies = []
    for k in range(1, plane):
        peer, dev = plane_peer(k)
        copy = remote(wg_s.at[peer], wg_r.at[my_p], wg_ss.at[k], wg_rs.at[k], dev)
        copy.start()
        wg_copies.append(copy)
    wg_r[my_p] = wg_s[my_p]

    gf_copies = []
    for k in range(1, groups):
        peer = group_peer(k)
        w_rows = weight_ref[pl.ds(pl.multiple_of(peer * fw, fw), fw), :]
        gf_ref[k] = mm_nt(q_ref_dy[...], w_rows).astype(BF16)
        copy = remote(gf_ref.at[k], gf_out.at[own_rows], gf_ss.at[k], gf_rs.at[k],
                      {"regroup": peer})
        copy.start()
        gf_copies.append(copy)
    w_rows = weight_ref[pl.ds(pl.multiple_of(my_g * fw, fw), fw), :]
    gf_ref[0] = mm_nt(q_ref_dy[...], w_rows).astype(BF16)
    gf_own = pltpu.make_async_copy(gf_ref.at[0], gf_out.at[own_rows], local_sem.at[1])
    gf_own.start()

    for copy in wg_copies:
        copy.wait_recv()
    piece = wg_r[0].astype(F32)
    for p in range(1, plane):
        piece = piece + wg_r[p].astype(F32)
    wz_ref[my_l] = piece.astype(wz_ref.dtype)
    wz_copies = []
    for k in range(1, loops):
        copy = remote(wz_ref.at[my_l], wz_ref.at[my_l], wz_ss.at[k], wz_rs.at[k],
                      {"loop": loop_peer(k)})
        copy.start()
        wz_copies.append(copy)
    for copy in wz_copies:
        copy.wait_recv()
    piece = wz_ref[0].astype(F32)
    for l in range(1, loops):
        piece = piece + wz_ref[l].astype(F32)
    wf_ref[my_p] = piece.astype(wf_ref.dtype)
    wf_copies = []
    for k in range(1, plane):
        copy = remote(wf_ref.at[my_p], wf_ref.at[my_p], wf_ss.at[k], wf_rs.at[k],
                      plane_peer(k)[1])
        copy.start()
        wf_copies.append(copy)
    for copy in wf_copies:
        copy.wait_recv()
    wf_copy = pltpu.make_async_copy(wf_ref, wf_out, local_sem.at[0])
    wf_copy.start()
    out_copy.wait()
    gf_own.wait()
    wf_copy.wait()
    for copy in gf_copies:
        copy.wait_recv()
    for copies in (feat_copies, deg_copies, part_copies, net_copies, gpart_copies, gnet_copies,
                   wg_copies, gf_copies, wz_copies, wf_copies):
        for copy in copies:
            copy.wait_send()


def store_kernel(scale, out_in, gf_in, wf_in, out_hbm, gf_hbm, gw_hbm, wf_ref, gw_ref, sem):
    load = pltpu.make_async_copy(wf_in, wf_ref, sem.at[3])
    load.start()
    copies = [
        pltpu.make_async_copy(out_in, out_hbm, sem.at[0]),
        pltpu.make_async_copy(gf_in, gf_hbm, sem.at[1]),
        pltpu.make_async_copy(gw_ref, gw_hbm, sem.at[2]),
    ]
    copies[0].start()
    copies[1].start()
    plane, rows_p, _ = wf_ref.shape
    load.wait()
    for p in range(plane):
        gw_ref[p * rows_p:(p + 1) * rows_p, :] = wf_ref[p].astype(F32) * scale
    copies[2].start()
    for copy in copies:
        copy.wait()


def per_device(groups, loops, replicas,
               features, weight, tiles, tile_row, tile_col, tile_width, cotangent):
    cells, chans = cotangent.shape[-2:]
    slots, edge = tiles.shape[-3:-1]
    total_rows, fw = features.shape[-2:]
    plane = groups * replicas
    rows_p = chans // plane
    link = BF16 if rows_p % 16 == 0 else F32
    anym = pl.BlockSpec(memory_space=pl.ANY)
    dma = pltpu.SemaphoreType.DMA
    V = pltpu.VMEM
    scratch = [
        pltpu.SMEM((slots,), jnp.int32), pltpu.SMEM((slots,), jnp.int32),
        pltpu.SMEM((slots,), jnp.int32), V((chans, chans), BF16),
        V((slots, edge, edge), BF16), V((cells, chans), BF16), V((groups, cells, fw), BF16),
        V((chans, cells), BF16), V((cells, 3 * edge), BF16), V((3 * edge, cells), BF16),
        V((cells, chans), F32), V((cells, chans), BF16), V((cells, chans), BF16),
        V((cells, chans), F32), V((cells, chans), F32),
        V((cells, chans), BF16), V((groups, cells, fw), BF16),
        V((3, edge, edge), BF16), V((2, edge, edge), BF16), V((edge, chans), F32),
        V((2, edge, chans), BF16), V((2, edge, chans), BF16), V((3, edge, chans), BF16),
        V((2, edge, chans), BF16), V((2, edge, chans), BF16), V((3, edge, chans), BF16),
        V((plane, rows_p, chans), link), V((plane, rows_p, chans), link),
        V((loops, rows_p, chans), link), V((plane, rows_p, chans), link),
        dma((8,)), dma((groups,)), dma((groups,)),
        dma((2,)), dma((2,)), dma((2,)), dma((2,)), dma((2,)), dma((2,)),
        dma((2,)), dma((2,)), dma((2,)), dma((2,)), dma((groups,)), dma((groups,)),
        dma((plane,)), dma((plane,)), dma((loops,)), dma((loops,)), dma((plane,)), dma((plane,)),
    ]
    out, gf, wf = pl.pallas_call(
        functools.partial(layer_kernel, groups, loops, replicas),
        out_shape=(
            jax.ShapeDtypeStruct((cells, chans), BF16),
            jax.ShapeDtypeStruct((total_rows, fw), BF16),
            jax.ShapeDtypeStruct((plane, rows_p, chans), link),
        ),
        in_specs=[anym] * 7,
        out_specs=(anym, anym, anym),
        scratch_shapes=scratch,
        compiler_params=pltpu.CompilerParams(
            collective_id=0, has_side_effects=True, vmem_limit_bytes=60 << 20),
    )(tile_row[0, 0, 0], tile_col[0, 0, 0], tile_width[0, 0, 0], features[0, 0], weight,
      tiles[0, 0, 0], cotangent[0, 0, 0])
    out, gf, gw = pl.pallas_call(
        functools.partial(store_kernel, 1.0 / math.sqrt(cells * plane * loops)),
        out_shape=(
            jax.ShapeDtypeStruct((cells, chans), BF16),
            jax.ShapeDtypeStruct((total_rows, fw), BF16),
            jax.ShapeDtypeStruct((chans, chans), F32),
        ),
        in_specs=[anym] * 3,
        out_specs=(anym, anym, anym),
        scratch_shapes=[V((plane, rows_p, chans), link), V((chans, chans), F32), dma((4,))],
        compiler_params=pltpu.CompilerParams(vmem_limit_bytes=60 << 20),
    )(out, gf, wf)
    return out[None, None, None], gf[None, None], gw


def solution(mesh):
    sizes = dict(mesh.shape)
    return jax.shard_map(
        functools.partial(per_device, sizes["regroup"], sizes["loop"], sizes["replica"]),
        mesh=mesh,
        in_specs=(
            P("replica", "loop", None, "regroup"),
            P(),
            P("replica", "loop", "regroup", None, None, None),
            P("replica", "loop", "regroup", None),
            P("replica", "loop", "regroup", None),
            P("replica", "loop", "regroup", None),
            P("replica", "loop", "regroup", None, None),
        ),
        out_specs=(
            P("replica", "loop", "regroup", None, None),
            P("replica", "loop", None, "regroup"),
            P(),
        ),
        check_vma=False,
    )
```

```python
import functools
import math

import jax
import jax.numpy as jnp
from jax import lax
from jax.experimental import pallas as pl
from jax.experimental.pallas import tpu as pltpu
from jax.sharding import PartitionSpec as P

EPSILON = 1e-06
MESH = pl.DeviceIdType.MESH
F32 = jnp.float32
BF16 = jnp.bfloat16


def mm(a, b):
    return jnp.dot(a, b, preferred_element_type=F32)


def mm_nt(a, b):
    return lax.dot_general(a, b, (((1,), (1,)), ((), ())), preferred_element_type=F32)


def layer_kernel(
    groups, loops, replicas,
    row_hbm, col_hbm, width_hbm, feat_hbm, weight_hbm, tiles_hbm, cot_hbm,
    out_hbm, gf_out, wf_out,
    row_ref, col_ref, width_ref, weight_ref, tiles_ref, sums_ref, own_ref, cot_ref, x_ref, xt_ref, h_ref, ht_ref, rs_ref, y_ref, q_ref, acc_ref, dpre_ref,
    out_ref, gf_ref, deg_s, deg_r, deinv_ref, part_s, part_r, net_ref, gpart_s, gpart_r, gnet_ref,
    wg_s, wg_r, wz_ref, wf_ref,
    local_sem, feat_ss, feat_rs, deg_ss, deg_rs, part_ss, part_rs, net_ss, net_rs,
    gpart_ss, gpart_rs, gnet_ss, gnet_rs, gf_ss, gf_rs, wg_ss, wg_rs, wz_ss, wz_rs, wf_ss, wf_rs,
):
    slots, edge, _ = tiles_hbm.shape
    cells, chans = cot_hbm.shape
    fw = feat_hbm.shape[1]
    plane = groups * replicas
    width = edge
    chunks = chans // width
    my_g = lax.axis_index("regroup")
    my_l = lax.axis_index("loop")
    my_r = lax.axis_index("replica")
    my_p = my_r * groups + my_g

    def group_peer(k):
        return lax.rem(my_g + k, groups)

    def loop_peer(k):
        return lax.rem(my_l + k, loops)

    def plane_peer(k):
        peer = lax.rem(my_p + k, plane)
        return peer, {"replica": lax.div(peer, groups), "regroup": lax.rem(peer, groups)}

    prev_dev = {"loop": loop_peer(loops - 1)}
    next_dev = {"loop": loop_peer(1)}

    def remote(src, dst, ss, rs, dev):
        return pltpu.make_async_remote_copy(
            src_ref=src, dst_ref=dst, send_sem=ss, recv_sem=rs, device_id=dev,
            device_id_type=MESH)

    barrier = pltpu.get_barrier_semaphore()
    for k in range(1, plane):
        pl.semaphore_signal(barrier, inc=1, device_id=plane_peer(k)[1], device_id_type=MESH)
    for k in range(1, loops):
        pl.semaphore_signal(barrier, inc=1, device_id={"loop": loop_peer(k)}, device_id_type=MESH)

    index_copies = [
        pltpu.make_async_copy(src, dst, local_sem.at[5 + i])
        for i, (src, dst) in enumerate(
            ((row_hbm, row_ref), (col_hbm, col_ref), (width_hbm, width_ref)))
    ]
    for copy in index_copies:
        copy.start()
    weight_copy = pltpu.make_async_copy(weight_hbm, weight_ref, local_sem.at[3])
    weight_copy.start()
    tiles_copy = pltpu.make_async_copy(tiles_hbm, tiles_ref, local_sem.at[0])
    tiles_copy.start()
    own_rows = pl.ds(pl.multiple_of(my_g * cells, cells), cells)
    own_copy = pltpu.make_async_copy(feat_hbm.at[own_rows], x_ref.at[my_g], local_sem.at[1])
    own_copy.start()
    cot_copy = pltpu.make_async_copy(cot_hbm, cot_ref, local_sem.at[2])
    cot_copy.start()

    pl.semaphore_wait(barrier, plane - 1 + loops - 1)

    feat_copies = []
    for k in range(1, groups):
        peer = group_peer(k)
        rows = pl.ds(pl.multiple_of(peer * cells, cells), cells)
        copy = remote(feat_hbm.at[rows], x_ref.at[my_g], feat_ss.at[k], feat_rs.at[k],
                      {"regroup": peer})
        copy.start()
        feat_copies.append(copy)

    for copy in index_copies:
        copy.wait()
    tiles_copy.wait()
    lane = lax.broadcasted_iota(jnp.int32, (1, edge), 1)
    blocks = cells // edge
    spots = 3 * blocks
    sums_ref[0] = jnp.zeros((edge, edge), F32)

    def add_tile(t, last):
        place = lax.rem(col_ref[t] - my_l + loops, loops)
        spot = row_ref[t] * 3 + jnp.where(place == 0, 1, jnp.where(place == 1, 2, 0))
        link = jnp.int32(0)
        for k in range(spots):
            link = jnp.where(spot == k, last[k], link)
        tile = jnp.where(lane < width_ref[t], tiles_ref[t].astype(F32), 0.0)
        sums_ref[t + 1] = tile + sums_ref[link]
        return tuple(jnp.where(spot == k, t + 1, last[k]) for k in range(spots))

    last = lax.fori_loop(0, slots, add_tile, (jnp.int32(0),) * spots, unroll=4)
    for b in range(blocks):
        for c in range(3):
            h_ref[b * edge:(b + 1) * edge, c * edge:(c + 1) * edge] = (
                sums_ref[last[b * 3 + c]].astype(BF16))
    for c in range(3):
        ht_ref[c * edge:(c + 1) * edge, :] = h_ref[:, c * edge:(c + 1) * edge].T

    deg_s[...] = mm(ht_ref[...], jnp.ones((cells, edge), BF16)).astype(BF16).reshape(3, edge, edge)
    deg_copies = [
        remote(deg_s.at[0], deg_r.at[1], deg_ss.at[0], deg_rs.at[1], prev_dev),
        remote(deg_s.at[2], deg_r.at[0], deg_ss.at[1], deg_rs.at[0], next_dev),
    ]
    for copy in deg_copies:
        copy.start()
    rs_ref[...] = lax.rsqrt(1.0 + mm(h_ref[...], jnp.ones((3 * edge, chans), BF16)))

    own_copy.wait()
    weight_copy.wait()
    for copy in feat_copies:
        copy.wait_recv()
    y32 = mm(x_ref[0], weight_ref[0:fw, :])
    for g in range(1, groups):
        y32 = y32 + mm(x_ref[g], weight_ref[g * fw:(g + 1) * fw, :])
    y16 = y32.astype(BF16)
    y_ref[...] = y16
    q_ref[...] = (y16.astype(F32) * rs_ref[...]).astype(BF16)

    def start_sums(send_buf, recv_buf, ss, rs):
        owns, copies = [], []
        for h in range(chunks):
            sums = mm(ht_ref[...], q_ref[:, h * width:(h + 1) * width])
            send_buf[h, 0] = sums[0:edge].astype(BF16)
            send_buf[h, 1] = sums[2 * edge:].astype(BF16)
            pair = (
                remote(send_buf.at[h, 0], recv_buf.at[h, 1], ss.at[h, 0], rs.at[h, 1], prev_dev),
                remote(send_buf.at[h, 1], recv_buf.at[h, 0], ss.at[h, 1], rs.at[h, 0], next_dev),
            )
            for copy in pair:
                copy.start()
            copies.append(pair)
            own_ref[:, h * width:(h + 1) * width] = sums[edge:2 * edge].astype(BF16)
        return copies

    def start_nets(copies, recv_buf, net, ss, rs):
        news = []
        for h in range(chunks):
            for copy in copies[h]:
                copy.wait_recv()
            total = (own_ref[:, h * width:(h + 1) * width].astype(F32)
                     + recv_buf[h, 0].astype(F32) + recv_buf[h, 1].astype(F32))
            net[h, 1] = (total * deinv_ref[:, 0:width]).astype(BF16)
            pair = (
                remote(net.at[h, 1], net.at[h, 2], ss.at[h, 0], rs.at[h, 1], prev_dev),
                remote(net.at[h, 1], net.at[h, 0], ss.at[h, 1], rs.at[h, 0], next_dev),
            )
            for copy in pair:
                copy.start()
            news.append(pair)
        return news

    def finish_nets(copies, net, h):
        for copy in copies[h]:
            copy.wait_recv()
        return mm(h_ref[...], net[h].reshape(3 * edge, width))

    part_copies = start_sums(part_s, part_r, part_ss, part_rs)
    for g in range(groups):
        xt_ref[g * fw:(g + 1) * fw, :] = x_ref[g].T
    for copy in deg_copies:
        copy.wait_recv()
    degree = (1.0 + deg_s[1].astype(F32) + deg_r[0].astype(F32) + deg_r[1].astype(F32))
    deinv_ref[...] = 1.0 / degree
    net_copies = start_nets(part_copies, part_r, net_ref, net_ss, net_rs)
    cot_copy.wait()
    for h in range(chunks):
        acc_ref[:, h * width:(h + 1) * width] = finish_nets(net_copies, net_ref, h)

    step = 64

    def middle(i, carry):
        rows = pl.ds(pl.multiple_of(i * step, step), step)
        root = rs_ref[rows, :]
        z = acc_ref[rows, :] * root
        inv = lax.rsqrt(jnp.mean(z * z, axis=-1, keepdims=True) + EPSILON)
        normed = z * inv
        pre = y_ref[rows, :].astype(F32) + normed
        sig = 1.0 / (1.0 + jnp.exp(-pre))
        out_ref[rows, :] = (pre * sig).astype(BF16)
        dpre = cot_ref[rows, :].astype(F32) * sig * (1.0 + pre * (1.0 - sig))
        dpre_ref[rows, :] = dpre
        dz = inv * (dpre - normed * jnp.mean(dpre * normed, axis=-1, keepdims=True))
        q_ref[rows, :] = (dz * root).astype(BF16)
        return carry

    lax.fori_loop(0, cells // step, middle, 0, unroll=2)
    out_copy = pltpu.make_async_copy(out_ref, out_hbm, local_sem.at[4])

    gpart_copies = start_sums(gpart_s, gpart_r, gpart_ss, gpart_rs)
    out_copy.start()
    gnet_copies = start_nets(gpart_copies, gpart_r, gnet_ref, gnet_ss, gnet_rs)

    rows_p = chans // plane
    wg_copies = []
    for h in range(chunks):
        cols = slice(h * width, (h + 1) * width)
        back = finish_nets(gnet_copies, gnet_ref, h)
        dy = (dpre_ref[:, cols] + back * rs_ref[:, cols]).astype(BF16)
        y_ref[:, cols] = dy
        wg = mm(xt_ref[...], dy)
        for p in range(plane):
            wg_s[h, p] = wg[p * rows_p:(p + 1) * rows_p].astype(wg_s.dtype)
        for k in range(1, plane):
            peer, dev = plane_peer(k)
            copy = remote(wg_s.at[h, peer], wg_r.at[h, my_p], wg_ss.at[h, k], wg_rs.at[h, k], dev)
            copy.start()
            wg_copies.append(copy)
        wg_r[h, my_p] = wg_s[h, my_p]

    gf_copies = []
    for k in range(groups):
        peer = group_peer(k)
        w_rows = weight_ref[pl.ds(pl.multiple_of(peer * fw, fw), fw), :]
        gf_ref[k] = mm_nt(y_ref[...], w_rows).astype(BF16)
        if k > 0:
            gf_copies.append(remote(gf_ref.at[k], gf_out.at[own_rows], gf_ss.at[k], gf_rs.at[k],
                                    {"regroup": peer}))
    gf_own = pltpu.make_async_copy(gf_ref.at[0], gf_out.at[own_rows], local_sem.at[1])
    gf_own.start()

    for copy in wg_copies:
        copy.wait_recv()
    for h in range(chunks):
        piece = wg_r[h, 0].astype(F32)
        for p in range(1, plane):
            piece = piece + wg_r[h, p].astype(F32)
        wz_ref[my_l, :, h * width:(h + 1) * width] = piece.astype(wz_ref.dtype)
    wz_copies = []
    for k in range(1, loops):
        copy = remote(wz_ref.at[my_l], wz_ref.at[my_l], wz_ss.at[k], wz_rs.at[k],
                      {"loop": loop_peer(k)})
        copy.start()
        wz_copies.append(copy)
    for copy in gf_copies:
        copy.start()
    for copy in wz_copies:
        copy.wait_recv()
    piece = wz_ref[0].astype(F32)
    for l in range(1, loops):
        piece = piece + wz_ref[l].astype(F32)
    wf_ref[my_p] = piece.astype(wf_ref.dtype)
    wf_copies = []
    for k in range(1, plane):
        copy = remote(wf_ref.at[my_p], wf_ref.at[my_p], wf_ss.at[k], wf_rs.at[k],
                      plane_peer(k)[1])
        copy.start()
        wf_copies.append(copy)
    for copy in wf_copies:
        copy.wait_recv()
    wf_copy = pltpu.make_async_copy(wf_ref, wf_out, local_sem.at[0])
    wf_copy.start()
    out_copy.wait()
    gf_own.wait()
    wf_copy.wait()
    for copy in gf_copies:
        copy.wait_recv()
    for copies in (feat_copies, deg_copies, wg_copies, gf_copies, wz_copies, wf_copies,
                   *part_copies, *net_copies, *gpart_copies, *gnet_copies):
        for copy in copies:
            copy.wait_send()


def store_kernel(scale, out_in, gf_in, wf_in, out_hbm, gf_hbm, gw_hbm,
                 out_ref, gf_ref, wf_ref, gw_ref, sem):
    loads = [
        pltpu.make_async_copy(out_in, out_ref, sem.at[3]),
        pltpu.make_async_copy(gf_in, gf_ref, sem.at[4]),
        pltpu.make_async_copy(wf_in, wf_ref, sem.at[5]),
    ]
    stores = [
        pltpu.make_async_copy(out_ref, out_hbm, sem.at[0]),
        pltpu.make_async_copy(gf_ref, gf_hbm, sem.at[1]),
        pltpu.make_async_copy(gw_ref, gw_hbm, sem.at[2]),
    ]
    for load in loads:
        load.start()
    plane, rows_p, _ = wf_ref.shape
    for load, store in zip(loads, stores):
        load.wait()
        if store is stores[2]:
            for p in range(plane):
                gw_ref[p * rows_p:(p + 1) * rows_p, :] = wf_ref[p].astype(F32) * scale
        store.start()
    for store in stores:
        store.wait()


def per_device(groups, loops, replicas,
               features, weight, tiles, tile_row, tile_col, tile_width, cotangent):
    cells, chans = cotangent.shape[-2:]
    slots, edge = tiles.shape[-3:-1]
    total_rows, fw = features.shape[-2:]
    plane = groups * replicas
    rows_p = chans // plane
    chunks = chans // edge
    link = BF16 if rows_p % 16 == 0 else F32
    anym = pl.BlockSpec(memory_space=pl.ANY)
    dma = pltpu.SemaphoreType.DMA
    V = pltpu.VMEM
    scratch = [
        pltpu.SMEM((slots,), jnp.int32), pltpu.SMEM((slots,), jnp.int32),
        pltpu.SMEM((slots,), jnp.int32), V((chans, chans), BF16),
        V((slots, edge, edge), BF16), V((slots + 1, edge, edge), F32), V((edge, chans), BF16),
        V((cells, chans), BF16), V((groups, cells, fw), BF16),
        V((chans, cells), BF16), V((cells, 3 * edge), BF16), V((3 * edge, cells), BF16),
        V((cells, chans), F32), V((cells, chans), BF16), V((cells, chans), BF16),
        V((cells, chans), F32), V((cells, chans), F32),
        V((cells, chans), BF16), V((groups, cells, fw), BF16),
        V((3, edge, edge), BF16), V((2, edge, edge), BF16), V((edge, edge), F32),
        *([V((chunks, 2, edge, edge), BF16)] * 2), V((chunks, 3, edge, edge), BF16),
        *([V((chunks, 2, edge, edge), BF16)] * 2), V((chunks, 3, edge, edge), BF16),
        *([V((chunks, plane, rows_p, edge), link)] * 2),
        V((loops, rows_p, chans), link), V((plane, rows_p, chans), link),
        dma((8,)), dma((groups,)), dma((groups,)), dma((2,)), dma((2,)),
        *([dma((chunks, 2))] * 8), dma((groups,)), dma((groups,)),
        *([dma((chunks, plane))] * 2), *([dma((loops,))] * 2), *([dma((plane,))] * 2),
    ]
    out, gf, wf = pl.pallas_call(
        functools.partial(layer_kernel, groups, loops, replicas),
        out_shape=(
            jax.ShapeDtypeStruct((cells, chans), BF16),
            jax.ShapeDtypeStruct((total_rows, fw), BF16),
            jax.ShapeDtypeStruct((plane, rows_p, chans), link),
        ),
        in_specs=[anym] * 7,
        out_specs=(anym, anym, anym),
        scratch_shapes=scratch,
        compiler_params=pltpu.CompilerParams(
            collective_id=0, has_side_effects=True, vmem_limit_bytes=60 << 20),
    )(tile_row[0, 0, 0], tile_col[0, 0, 0], tile_width[0, 0, 0], features[0, 0], weight,
      tiles[0, 0, 0], cotangent[0, 0, 0])
    out, gf, gw = pl.pallas_call(
        functools.partial(store_kernel, 1.0 / math.sqrt(cells * plane * loops)),
        out_shape=(
            jax.ShapeDtypeStruct((cells, chans), BF16),
            jax.ShapeDtypeStruct((total_rows, fw), BF16),
            jax.ShapeDtypeStruct((chans, chans), F32),
        ),
        in_specs=[anym] * 3,
        out_specs=(anym, anym, anym),
        scratch_shapes=[
            V((cells, chans), BF16), V((total_rows, fw), BF16), V((plane, rows_p, chans), link),
            V((chans, chans), F32), dma((6,)),
        ],
        compiler_params=pltpu.CompilerParams(vmem_limit_bytes=60 << 20),
    )(out, gf, wf)
    return out[None, None, None], gf[None, None], gw


def solution(mesh):
    sizes = dict(mesh.shape)
    return jax.shard_map(
        functools.partial(per_device, sizes["regroup"], sizes["loop"], sizes["replica"]),
        mesh=mesh,
        in_specs=(
            P("replica", "loop", None, "regroup"),
            P(),
            P("replica", "loop", "regroup", None, None, None),
            P("replica", "loop", "regroup", None),
            P("replica", "loop", "regroup", None),
            P("replica", "loop", "regroup", None),
            P("replica", "loop", "regroup", None, None),
        ),
        out_specs=(
            P("replica", "loop", "regroup", None, None),
            P("replica", "loop", None, "regroup"),
            P(),
        ),
        check_vma=False,
    )
```

```python
import functools
import math

import jax
import jax.numpy as jnp
from jax import lax
from jax.experimental import pallas as pl
from jax.experimental.pallas import tpu as pltpu
from jax.sharding import PartitionSpec as P

EPSILON = 1e-06
MESH = pl.DeviceIdType.MESH
F32 = jnp.float32
BF16 = jnp.bfloat16


def mm(a, b):
    return jnp.dot(a, b, preferred_element_type=F32)


def mm_nt(a, b):
    return lax.dot_general(a, b, (((1,), (1,)), ((), ())), preferred_element_type=F32)


def layer_kernel(
    groups, loops, replicas,
    row_hbm, col_hbm, width_hbm, feat_hbm, weight_hbm, tiles_hbm, cot_hbm,
    out_hbm, gf_out, wf_out,
    row_ref, col_ref, width_ref, weight_ref, tiles_ref, sums_ref, own_ref, usum_ref, ut_ref, direct_ref, cot_ref, x_ref, xt_ref, h_ref, ht_ref, rs_ref, y_ref, q_ref, acc_ref, dpre_ref,
    out_ref, gf_ref, deg_s, deg_r, deinv_ref, part_s, part_r, net_ref, gpart_s, gpart_r, gnet_ref,
    wg_s, wg_r, wz_ref, wf_ref,
    local_sem, feat_ss, feat_rs, deg_ss, deg_rs, part_ss, part_rs, net_ss, net_rs,
    gpart_ss, gpart_rs, gnet_ss, gnet_rs, gf_ss, gf_rs, wg_ss, wg_rs, wz_ss, wz_rs, wf_ss, wf_rs,
):
    slots, edge, _ = tiles_hbm.shape
    cells, chans = cot_hbm.shape
    fw = feat_hbm.shape[1]
    plane = groups * replicas
    width = edge
    chunks = chans // width
    my_g = lax.axis_index("regroup")
    my_l = lax.axis_index("loop")
    my_r = lax.axis_index("replica")
    my_p = my_r * groups + my_g

    def group_peer(k):
        return lax.rem(my_g + k, groups)

    def loop_peer(k):
        return lax.rem(my_l + k, loops)

    def plane_peer(k):
        peer = lax.rem(my_p + k, plane)
        return peer, {"replica": lax.div(peer, groups), "regroup": lax.rem(peer, groups)}

    prev_dev = {"loop": loop_peer(loops - 1)}
    next_dev = {"loop": loop_peer(1)}

    def remote(src, dst, ss, rs, dev):
        return pltpu.make_async_remote_copy(
            src_ref=src, dst_ref=dst, send_sem=ss, recv_sem=rs, device_id=dev,
            device_id_type=MESH)

    barrier = pltpu.get_barrier_semaphore()
    for k in range(1, plane):
        pl.semaphore_signal(barrier, inc=1, device_id=plane_peer(k)[1], device_id_type=MESH)
    for k in range(1, loops):
        pl.semaphore_signal(barrier, inc=1, device_id={"loop": loop_peer(k)}, device_id_type=MESH)

    index_copies = [
        pltpu.make_async_copy(src, dst, local_sem.at[5 + i])
        for i, (src, dst) in enumerate(
            ((row_hbm, row_ref), (col_hbm, col_ref), (width_hbm, width_ref)))
    ]
    for copy in index_copies:
        copy.start()
    weight_copy = pltpu.make_async_copy(weight_hbm, weight_ref, local_sem.at[3])
    weight_copy.start()
    tiles_copy = pltpu.make_async_copy(tiles_hbm, tiles_ref, local_sem.at[0])
    tiles_copy.start()
    own_rows = pl.ds(pl.multiple_of(my_g * cells, cells), cells)
    own_copy = pltpu.make_async_copy(feat_hbm.at[own_rows], x_ref.at[my_g], local_sem.at[1])
    own_copy.start()
    cot_copy = pltpu.make_async_copy(cot_hbm, cot_ref, local_sem.at[2])
    cot_copy.start()

    pl.semaphore_wait(barrier, plane - 1 + loops - 1)

    feat_copies = []
    for k in range(1, groups):
        peer = group_peer(k)
        rows = pl.ds(pl.multiple_of(peer * cells, cells), cells)
        copy = remote(feat_hbm.at[rows], x_ref.at[my_g], feat_ss.at[k], feat_rs.at[k],
                      {"regroup": peer})
        copy.start()
        feat_copies.append(copy)

    for copy in index_copies:
        copy.wait()
    tiles_copy.wait()
    lane = lax.broadcasted_iota(jnp.int32, (1, edge), 1)
    blocks = cells // edge
    spots = 3 * blocks
    sums_ref[0] = jnp.zeros((edge, edge), F32)

    def add_tile(t, last):
        place = lax.rem(col_ref[t] - my_l + loops, loops)
        spot = row_ref[t] * 3 + jnp.where(place == 0, 1, jnp.where(place == 1, 2, 0))
        link = jnp.int32(0)
        for k in range(spots):
            link = jnp.where(spot == k, last[k], link)
        tile = jnp.where(lane < width_ref[t], tiles_ref[t].astype(F32), 0.0)
        sums_ref[t + 1] = tile + sums_ref[link]
        return tuple(jnp.where(spot == k, t + 1, last[k]) for k in range(spots))

    last = lax.fori_loop(0, slots, add_tile, (jnp.int32(0),) * spots, unroll=4)
    for b in range(blocks):
        for c in range(3):
            h_ref[b * edge:(b + 1) * edge, c * edge:(c + 1) * edge] = (
                sums_ref[last[b * 3 + c]].astype(BF16))
    for c in range(3):
        ht_ref[c * edge:(c + 1) * edge, :] = h_ref[:, c * edge:(c + 1) * edge].T

    deg_s[...] = mm(ht_ref[...], jnp.ones((cells, edge), BF16)).astype(BF16).reshape(3, edge, edge)
    deg_copies = [
        remote(deg_s.at[0], deg_r.at[1], deg_ss.at[0], deg_rs.at[1], prev_dev),
        remote(deg_s.at[2], deg_r.at[0], deg_ss.at[1], deg_rs.at[0], next_dev),
    ]
    for copy in deg_copies:
        copy.start()
    rs_ref[...] = lax.rsqrt(1.0 + mm(h_ref[...], jnp.ones((3 * edge, chans), BF16)))

    weight_copy.wait()
    own_copy.wait()

    def group_rows(k):
        source = lax.rem(my_g + groups - k, groups)
        return source, pl.ds(pl.multiple_of(source * fw, fw), fw)

    def send_sums(sums, send, recv, ss, rs):
        send[0] = sums[0:edge].astype(BF16)
        send[1] = sums[2 * edge:].astype(BF16)
        pair = (
            remote(send.at[0], recv.at[1], ss.at[0], rs.at[1], prev_dev),
            remote(send.at[1], recv.at[0], ss.at[1], rs.at[0], next_dev),
        )
        for copy in pair:
            copy.start()
        return pair

    part_copies = []
    for k in range(groups):
        source, _ = group_rows(k)
        if k > 0:
            feat_copies[k - 1].wait_recv()
        xs = (x_ref[source].astype(F32) * rs_ref[:, 0:fw]).astype(BF16)
        sums = mm(ht_ref[...], xs)
        part_copies.append(send_sums(
            sums, part_s.at[k], part_r.at[k], part_ss.at[k], part_rs.at[k]))
        usum_ref[k] = sums[edge:2 * edge].astype(BF16)

    y32 = mm(x_ref[0], weight_ref[0:fw, :])
    for g in range(1, groups):
        y32 = y32 + mm(x_ref[g], weight_ref[g * fw:(g + 1) * fw, :])
    y_ref[...] = y32.astype(BF16)

    def send_nets(net, ss, rs):
        pair = (
            remote(net.at[1], net.at[2], ss.at[0], rs.at[1], prev_dev),
            remote(net.at[1], net.at[0], ss.at[1], rs.at[0], next_dev),
        )
        for copy in pair:
            copy.start()
        return pair

    def finish_nets(copies, net, h):
        for copy in copies[h]:
            copy.wait_recv()
        return mm(h_ref[...], net[h].reshape(3 * edge, width))

    for g in range(groups):
        xt_ref[g * fw:(g + 1) * fw, :] = x_ref[g].T
    for copy in deg_copies:
        copy.wait_recv()
    degree = (1.0 + deg_s[1].astype(F32) + deg_r[0].astype(F32) + deg_r[1].astype(F32))
    deinv_ref[...] = 1.0 / degree
    nets = None
    for k in range(groups):
        _, rows = group_rows(k)
        for copy in part_copies[k]:
            copy.wait_recv()
        total = (usum_ref[k].astype(F32) + part_r[k, 0].astype(F32) + part_r[k, 1].astype(F32)
                 ).astype(BF16)
        usum_ref[k] = total
        term = mm(total, weight_ref[rows, :])
        nets = term if nets is None else nets + term
    net_copies = []
    for h in range(chunks):
        net_ref[h, 1] = (nets[:, h * width:(h + 1) * width] * deinv_ref[...]).astype(BF16)
        net_copies.append(send_nets(net_ref.at[h], net_ss.at[h], net_rs.at[h]))
    for k in range(groups):
        _, rows = group_rows(k)
        ut_ref[rows, :] = usum_ref[k].T
    cot_copy.wait()
    for h in range(chunks):
        acc_ref[:, h * width:(h + 1) * width] = finish_nets(net_copies, net_ref, h)

    step = 64

    def middle(i, carry):
        rows = pl.ds(pl.multiple_of(i * step, step), step)
        root = rs_ref[rows, :]
        z = acc_ref[rows, :] * root
        inv = lax.rsqrt(jnp.mean(z * z, axis=-1, keepdims=True) + EPSILON)
        normed = z * inv
        pre = y_ref[rows, :].astype(F32) + normed
        sig = 1.0 / (1.0 + jnp.exp(-pre))
        out_ref[rows, :] = (pre * sig).astype(BF16)
        dpre = cot_ref[rows, :].astype(F32) * sig * (1.0 + pre * (1.0 - sig))
        dpre_ref[rows, :] = dpre
        dz = inv * (dpre - normed * jnp.mean(dpre * normed, axis=-1, keepdims=True))
        q_ref[rows, :] = (dz * root).astype(BF16)
        return carry

    lax.fori_loop(0, cells // step, middle, 0, unroll=2)
    out_copy = pltpu.make_async_copy(out_ref, out_hbm, local_sem.at[4])

    gpart_copies = []
    for h in range(chunks):
        cols = slice(h * width, (h + 1) * width)
        sums = mm(ht_ref[...], q_ref[:, cols])
        gpart_copies.append(send_sums(
            sums, gpart_s.at[h], gpart_r.at[h], gpart_ss.at[h], gpart_rs.at[h]))
        own_ref[:, cols] = sums[edge:2 * edge].astype(BF16)
    out_copy.start()

    rows_p = chans // plane
    direct_ref[...] = mm(xt_ref[...], dpre_ref[...].astype(BF16))
    gnet_copies, wg_copies = [], []
    for h in range(chunks):
        cols = slice(h * width, (h + 1) * width)
        for copy in gpart_copies[h]:
            copy.wait_recv()
        total = (own_ref[:, cols].astype(F32)
                 + gpart_r[h, 0].astype(F32) + gpart_r[h, 1].astype(F32))
        gnet_ref[h, 1] = (total * deinv_ref[...]).astype(BF16)
        gnet_copies.append(send_nets(gnet_ref.at[h], gnet_ss.at[h], gnet_rs.at[h]))
        wg = direct_ref[:, cols] + mm(ut_ref[...], gnet_ref[h, 1])
        for p in range(plane):
            wg_s[h, p] = wg[p * rows_p:(p + 1) * rows_p].astype(wg_s.dtype)
        for k in range(1, plane):
            peer, dev = plane_peer(k)
            copy = remote(wg_s.at[h, peer], wg_r.at[h, my_p], wg_ss.at[h, k], wg_rs.at[h, k], dev)
            copy.start()
            wg_copies.append(copy)
        wg_r[h, my_p] = wg_s[h, my_p]

    def finish_grad(h):
        cols = slice(h * width, (h + 1) * width)
        back = finish_nets(gnet_copies, gnet_ref, h)
        y_ref[:, cols] = (dpre_ref[:, cols] + back * rs_ref[:, cols]).astype(BF16)

    for h in range(chunks - 1):
        finish_grad(h)

    for copy in wg_copies:
        copy.wait_recv()
    for h in range(chunks):
        piece = wg_r[h, 0].astype(F32)
        for p in range(1, plane):
            piece = piece + wg_r[h, p].astype(F32)
        wz_ref[my_l, :, h * width:(h + 1) * width] = piece.astype(wz_ref.dtype)
    wz_copies = []
    for k in range(1, loops):
        copy = remote(wz_ref.at[my_l], wz_ref.at[my_l], wz_ss.at[k], wz_rs.at[k],
                      {"loop": loop_peer(k)})
        copy.start()
        wz_copies.append(copy)
    finish_grad(chunks - 1)
    gf_copies = []
    for k in [*range(1, groups), 0]:
        peer = group_peer(k)
        w_rows = weight_ref[pl.ds(pl.multiple_of(peer * fw, fw), fw), :]
        gf_ref[k] = mm_nt(y_ref[...], w_rows).astype(BF16)
        if k > 0:
            copy = remote(gf_ref.at[k], gf_out.at[own_rows], gf_ss.at[k], gf_rs.at[k],
                          {"regroup": peer})
            copy.start()
            gf_copies.append(copy)
    gf_own = pltpu.make_async_copy(gf_ref.at[0], gf_out.at[own_rows], local_sem.at[1])
    gf_own.start()

    for copy in wz_copies:
        copy.wait_recv()
    piece = wz_ref[0].astype(F32)
    for l in range(1, loops):
        piece = piece + wz_ref[l].astype(F32)
    wf_ref[my_p] = piece.astype(wf_ref.dtype)
    wf_copies = []
    for k in range(1, plane):
        copy = remote(wf_ref.at[my_p], wf_ref.at[my_p], wf_ss.at[k], wf_rs.at[k],
                      plane_peer(k)[1])
        copy.start()
        wf_copies.append(copy)
    for copy in wf_copies:
        copy.wait_recv()
    wf_copy = pltpu.make_async_copy(wf_ref, wf_out, local_sem.at[0])
    wf_copy.start()
    out_copy.wait()
    gf_own.wait()
    wf_copy.wait()
    for copy in gf_copies:
        copy.wait_recv()
    for copies in (feat_copies, deg_copies, wg_copies, gf_copies, wz_copies, wf_copies,
                   *part_copies, *net_copies, *gpart_copies, *gnet_copies):
        for copy in copies:
            copy.wait_send()


def store_kernel(scale, out_in, gf_in, wf_in, out_hbm, gf_hbm, gw_hbm,
                 out_ref, gf_ref, wf_ref, gw_ref, sem):
    loads = [
        pltpu.make_async_copy(out_in, out_ref, sem.at[3]),
        pltpu.make_async_copy(gf_in, gf_ref, sem.at[4]),
        pltpu.make_async_copy(wf_in, wf_ref, sem.at[5]),
    ]
    stores = [
        pltpu.make_async_copy(out_ref, out_hbm, sem.at[0]),
        pltpu.make_async_copy(gf_ref, gf_hbm, sem.at[1]),
        pltpu.make_async_copy(gw_ref, gw_hbm, sem.at[2]),
    ]
    for load in loads:
        load.start()
    plane, rows_p, _ = wf_ref.shape
    for load, store in zip(loads, stores):
        load.wait()
        if store is stores[2]:
            for p in range(plane):
                gw_ref[p * rows_p:(p + 1) * rows_p, :] = wf_ref[p].astype(F32) * scale
        store.start()
    for store in stores:
        store.wait()


def per_device(groups, loops, replicas,
               features, weight, tiles, tile_row, tile_col, tile_width, cotangent):
    cells, chans = cotangent.shape[-2:]
    slots, edge = tiles.shape[-3:-1]
    total_rows, fw = features.shape[-2:]
    plane = groups * replicas
    rows_p = chans // plane
    chunks = chans // edge
    link = BF16 if rows_p % 16 == 0 else F32
    anym = pl.BlockSpec(memory_space=pl.ANY)
    dma = pltpu.SemaphoreType.DMA
    V = pltpu.VMEM
    scratch = [
        pltpu.SMEM((slots,), jnp.int32), pltpu.SMEM((slots,), jnp.int32),
        pltpu.SMEM((slots,), jnp.int32), V((chans, chans), BF16),
        V((slots, edge, edge), BF16), V((slots + 1, edge, edge), F32), V((edge, chans), BF16),
        V((groups, edge, fw), BF16), V((chans, edge), BF16), V((chans, chans), F32),
        V((cells, chans), BF16), V((groups, cells, fw), BF16),
        V((chans, cells), BF16), V((cells, 3 * edge), BF16), V((3 * edge, cells), BF16),
        V((cells, chans), F32), V((cells, chans), BF16), V((cells, chans), BF16),
        V((cells, chans), F32), V((cells, chans), F32),
        V((cells, chans), BF16), V((groups, cells, fw), BF16),
        V((3, edge, edge), BF16), V((2, edge, edge), BF16), V((edge, edge), F32),
        *([V((groups, 2, edge, fw), BF16)] * 2), V((chunks, 3, edge, edge), BF16),
        *([V((chunks, 2, edge, edge), BF16)] * 2), V((chunks, 3, edge, edge), BF16),
        *([V((chunks, plane, rows_p, edge), link)] * 2),
        V((loops, rows_p, chans), link), V((plane, rows_p, chans), link),
        dma((8,)), dma((groups,)), dma((groups,)), dma((2,)), dma((2,)),
        *([dma((groups, 2))] * 2), *([dma((chunks, 2))] * 6), dma((groups,)), dma((groups,)),
        *([dma((chunks, plane))] * 2), *([dma((loops,))] * 2), *([dma((plane,))] * 2),
    ]
    out, gf, wf = pl.pallas_call(
        functools.partial(layer_kernel, groups, loops, replicas),
        out_shape=(
            jax.ShapeDtypeStruct((cells, chans), BF16),
            jax.ShapeDtypeStruct((total_rows, fw), BF16),
            jax.ShapeDtypeStruct((plane, rows_p, chans), link),
        ),
        in_specs=[anym] * 7,
        out_specs=(anym, anym, anym),
        scratch_shapes=scratch,
        compiler_params=pltpu.CompilerParams(
            collective_id=0, has_side_effects=True, vmem_limit_bytes=60 << 20),
    )(tile_row[0, 0, 0], tile_col[0, 0, 0], tile_width[0, 0, 0], features[0, 0], weight,
      tiles[0, 0, 0], cotangent[0, 0, 0])
    out, gf, gw = pl.pallas_call(
        functools.partial(store_kernel, 1.0 / math.sqrt(cells * plane * loops)),
        out_shape=(
            jax.ShapeDtypeStruct((cells, chans), BF16),
            jax.ShapeDtypeStruct((total_rows, fw), BF16),
            jax.ShapeDtypeStruct((chans, chans), F32),
        ),
        in_specs=[anym] * 3,
        out_specs=(anym, anym, anym),
        scratch_shapes=[
            V((cells, chans), BF16), V((total_rows, fw), BF16), V((plane, rows_p, chans), link),
            V((chans, chans), F32), dma((6,)),
        ],
        compiler_params=pltpu.CompilerParams(vmem_limit_bytes=60 << 20),
    )(out, gf, wf)
    return out[None, None, None], gf[None, None], gw


def solution(mesh):
    sizes = dict(mesh.shape)
    return jax.shard_map(
        functools.partial(per_device, sizes["regroup"], sizes["loop"], sizes["replica"]),
        mesh=mesh,
        in_specs=(
            P("replica", "loop", None, "regroup"),
            P(),
            P("replica", "loop", "regroup", None, None, None),
            P("replica", "loop", "regroup", None),
            P("replica", "loop", "regroup", None),
            P("replica", "loop", "regroup", None),
            P("replica", "loop", "regroup", None, None),
        ),
        out_specs=(
            P("replica", "loop", "regroup", None, None),
            P("replica", "loop", None, "regroup"),
            P(),
        ),
        check_vma=False,
    )
```

```python
import functools
import math

import jax
import jax.numpy as jnp
from jax import lax
from jax.experimental import pallas as pl
from jax.experimental.pallas import tpu as pltpu
from jax.sharding import PartitionSpec as P

EPSILON = 1e-06
MESH = pl.DeviceIdType.MESH
F32 = jnp.float32
BF16 = jnp.bfloat16


def mm(a, b):
    return jnp.dot(a, b, preferred_element_type=F32)


def mm_nt(a, b):
    return lax.dot_general(a, b, (((1,), (1,)), ((), ())), preferred_element_type=F32)


def layer_kernel(
    groups, loops, replicas,
    row_hbm, col_hbm, width_hbm, feat_hbm, weight_hbm, tiles_hbm, cot_hbm,
    out_hbm, gf_out, wf_out,
    row_ref, col_ref, width_ref, weight_ref, tiles_ref, sums_ref, own_ref, usum_ref, ut_ref, direct_ref, cot_ref, x_ref, xt_ref, h_ref, ht_ref, rs_ref, y_ref, q_ref, acc_ref, dpre_ref,
    out_ref, gf_ref, deg_s, deg_r, deinv_ref, part_s, part_r, net_ref, gpart_s, gpart_r, gnet_ref,
    wg_s, wg_r, wz_ref, wf_ref,
    local_sem, feat_ss, feat_rs, deg_ss, deg_rs, part_ss, part_rs, net_ss, net_rs,
    gpart_ss, gpart_rs, gnet_ss, gnet_rs, gf_ss, gf_rs, wg_ss, wg_rs, wz_ss, wz_rs, wf_ss, wf_rs,
):
    slots, edge, _ = tiles_hbm.shape
    cells, chans = cot_hbm.shape
    fw = feat_hbm.shape[1]
    plane = groups * replicas
    width = edge
    chunks = chans // width
    my_g = lax.axis_index("regroup")
    my_l = lax.axis_index("loop")
    my_r = lax.axis_index("replica")
    my_p = my_r * groups + my_g

    def group_peer(k):
        return lax.rem(my_g + k, groups)

    def loop_peer(k):
        return lax.rem(my_l + k, loops)

    def plane_peer(k):
        peer = lax.rem(my_p + k, plane)
        return peer, {"replica": lax.div(peer, groups), "regroup": lax.rem(peer, groups)}

    prev_dev = {"loop": loop_peer(loops - 1)}
    next_dev = {"loop": loop_peer(1)}
    wraps_up = lax.div(my_l + 1, loops)
    ways = [
        (d, {"loop": loop_peer((1 - d) * (loops - 1) + d)}) for d in (wraps_up, 1 - wraps_up)
    ]

    def remote(src, dst, ss, rs, dev):
        return pltpu.make_async_remote_copy(
            src_ref=src, dst_ref=dst, send_sem=ss, recv_sem=rs, device_id=dev,
            device_id_type=MESH)

    barrier = pltpu.get_barrier_semaphore()
    for k in range(1, plane):
        pl.semaphore_signal(barrier, inc=1, device_id=plane_peer(k)[1], device_id_type=MESH)
    for k in range(1, loops):
        pl.semaphore_signal(barrier, inc=1, device_id={"loop": loop_peer(k)}, device_id_type=MESH)

    index_copies = [
        pltpu.make_async_copy(src, dst, local_sem.at[5 + i])
        for i, (src, dst) in enumerate(
            ((row_hbm, row_ref), (col_hbm, col_ref), (width_hbm, width_ref)))
    ]
    for copy in index_copies:
        copy.start()
    weight_copy = pltpu.make_async_copy(weight_hbm, weight_ref, local_sem.at[3])
    weight_copy.start()
    tiles_copy = pltpu.make_async_copy(tiles_hbm, tiles_ref, local_sem.at[0])
    tiles_copy.start()
    own_rows = pl.ds(pl.multiple_of(my_g * cells, cells), cells)
    own_copy = pltpu.make_async_copy(feat_hbm.at[own_rows], x_ref.at[my_g], local_sem.at[1])
    own_copy.start()
    cot_copy = pltpu.make_async_copy(cot_hbm, cot_ref, local_sem.at[2])
    cot_copy.start()

    pl.semaphore_wait(barrier, plane - 1 + loops - 1)

    feat_copies = []
    for k in range(1, groups):
        peer = group_peer(k)
        rows = pl.ds(pl.multiple_of(peer * cells, cells), cells)
        copy = remote(feat_hbm.at[rows], x_ref.at[my_g], feat_ss.at[k], feat_rs.at[k],
                      {"regroup": peer})
        copy.start()
        feat_copies.append(copy)

    for copy in index_copies:
        copy.wait()
    tiles_copy.wait()
    lane = lax.broadcasted_iota(jnp.int32, (1, edge), 1)
    blocks = cells // edge
    spots = 3 * blocks
    sums_ref[0] = jnp.zeros((edge, edge), F32)

    def add_tile(t, last):
        place = lax.rem(col_ref[t] - my_l + loops, loops)
        spot = row_ref[t] * 3 + jnp.where(place == 0, 1, jnp.where(place == 1, 2, 0))
        link = jnp.int32(0)
        for k in range(spots):
            link = jnp.where(spot == k, last[k], link)
        tile = jnp.where(lane < width_ref[t], tiles_ref[t].astype(F32), 0.0)
        sums_ref[t + 1] = tile + sums_ref[link]
        return tuple(jnp.where(spot == k, t + 1, last[k]) for k in range(spots))

    last = lax.fori_loop(0, slots, add_tile, (jnp.int32(0),) * spots, unroll=4)
    for b in range(blocks):
        for c in range(3):
            h_ref[b * edge:(b + 1) * edge, c * edge:(c + 1) * edge] = (
                sums_ref[last[b * 3 + c]].astype(BF16))
    for c in range(3):
        ht_ref[c * edge:(c + 1) * edge, :] = h_ref[:, c * edge:(c + 1) * edge].T

    deg_s[...] = mm(ht_ref[...], jnp.ones((cells, edge), BF16)).astype(BF16).reshape(3, edge, edge)
    deg_copies = [
        remote(deg_s.at[0], deg_r.at[1], deg_ss.at[0], deg_rs.at[1], prev_dev),
        remote(deg_s.at[2], deg_r.at[0], deg_ss.at[1], deg_rs.at[0], next_dev),
    ]
    for copy in deg_copies:
        copy.start()
    rs_ref[...] = lax.rsqrt(1.0 + mm(h_ref[...], jnp.ones((3 * edge, chans), BF16)))

    weight_copy.wait()
    own_copy.wait()

    def group_rows(k):
        source = lax.rem(my_g + groups - k, groups)
        return source, pl.ds(pl.multiple_of(source * fw, fw), fw)

    def send_sums(sums, send, recv, ss, rs):
        send[0] = sums[0:edge].astype(BF16)
        send[1] = sums[2 * edge:].astype(BF16)
        pair = [
            remote(send.at[d], recv.at[1 - d], ss.at[d], rs.at[1 - d], dev) for d, dev in ways
        ]
        for copy in pair:
            copy.start()
        return pair

    part_copies = []
    for k in range(groups):
        source, _ = group_rows(k)
        if k > 0:
            feat_copies[k - 1].wait_recv()
        xs = (x_ref[source].astype(F32) * rs_ref[:, 0:fw]).astype(BF16)
        sums = mm(ht_ref[...], xs)
        part_copies.append(send_sums(
            sums, part_s.at[k], part_r.at[k], part_ss.at[k], part_rs.at[k]))
        usum_ref[k] = sums[edge:2 * edge].astype(BF16)

    y32 = mm(x_ref[0], weight_ref[0:fw, :])
    for g in range(1, groups):
        y32 = y32 + mm(x_ref[g], weight_ref[g * fw:(g + 1) * fw, :])
    y_ref[...] = y32.astype(BF16)

    def send_nets(net, ss, rs):
        pair = [
            remote(net.at[1], net.at[2 - 2 * d], ss.at[d], rs.at[1 - d], dev) for d, dev in ways
        ]
        for copy in pair:
            copy.start()
        return pair

    def finish_nets(copies, net, h):
        for copy in copies[h]:
            copy.wait_recv()
        return mm(h_ref[...], net[h].reshape(3 * edge, width))

    for g in range(groups):
        xt_ref[g * fw:(g + 1) * fw, :] = x_ref[g].T
    for copy in deg_copies:
        copy.wait_recv()
    degree = (1.0 + deg_s[1].astype(F32) + deg_r[0].astype(F32) + deg_r[1].astype(F32))
    deinv_ref[...] = 1.0 / degree
    nets = None
    for k in range(groups):
        _, rows = group_rows(k)
        for copy in part_copies[k]:
            copy.wait_recv()
        total = (usum_ref[k].astype(F32) + part_r[k, 0].astype(F32) + part_r[k, 1].astype(F32)
                 ).astype(BF16)
        usum_ref[k] = total
        term = mm(total, weight_ref[rows, :])
        nets = term if nets is None else nets + term
    net_copies = []
    for h in range(chunks):
        net_ref[h, 1] = (nets[:, h * width:(h + 1) * width] * deinv_ref[...]).astype(BF16)
        net_copies.append(send_nets(net_ref.at[h], net_ss.at[h], net_rs.at[h]))
    for k in range(groups):
        _, rows = group_rows(k)
        ut_ref[rows, :] = usum_ref[k].T
    cot_copy.wait()
    for h in range(chunks):
        acc_ref[:, h * width:(h + 1) * width] = finish_nets(net_copies, net_ref, h)

    step = 64

    def middle(i, carry):
        rows = pl.ds(pl.multiple_of(i * step, step), step)
        root = rs_ref[rows, :]
        z = acc_ref[rows, :] * root
        inv = lax.rsqrt(jnp.mean(z * z, axis=-1, keepdims=True) + EPSILON)
        normed = z * inv
        pre = y_ref[rows, :].astype(F32) + normed
        sig = 1.0 / (1.0 + jnp.exp(-pre))
        out_ref[rows, :] = (pre * sig).astype(BF16)
        dpre = cot_ref[rows, :].astype(F32) * sig * (1.0 + pre * (1.0 - sig))
        dpre_ref[rows, :] = dpre
        dz = inv * (dpre - normed * jnp.mean(dpre * normed, axis=-1, keepdims=True))
        q_ref[rows, :] = (dz * root).astype(BF16)
        return carry

    lax.fori_loop(0, cells // step, middle, 0, unroll=2)
    out_copy = pltpu.make_async_copy(out_ref, out_hbm, local_sem.at[4])

    gpart_copies = []
    for h in range(chunks):
        cols = slice(h * width, (h + 1) * width)
        sums = mm(ht_ref[...], q_ref[:, cols])
        gpart_copies.append(send_sums(
            sums, gpart_s.at[h], gpart_r.at[h], gpart_ss.at[h], gpart_rs.at[h]))
        own_ref[:, cols] = sums[edge:2 * edge].astype(BF16)
    out_copy.start()

    rows_p = chans // plane
    direct_ref[...] = mm(xt_ref[...], dpre_ref[...].astype(BF16))
    gnet_copies, wg_copies = [], []
    for h in range(chunks):
        cols = slice(h * width, (h + 1) * width)
        for copy in gpart_copies[h]:
            copy.wait_recv()
        total = (own_ref[:, cols].astype(F32)
                 + gpart_r[h, 0].astype(F32) + gpart_r[h, 1].astype(F32))
        gnet_ref[h, 1] = (total * deinv_ref[...]).astype(BF16)
        gnet_copies.append(send_nets(gnet_ref.at[h], gnet_ss.at[h], gnet_rs.at[h]))
        wg = direct_ref[:, cols] + mm(ut_ref[...], gnet_ref[h, 1])
        for p in range(plane):
            wg_s[h, p] = wg[p * rows_p:(p + 1) * rows_p].astype(wg_s.dtype)
        for k in range(1, plane):
            peer, dev = plane_peer(k)
            copy = remote(wg_s.at[h, peer], wg_r.at[h, my_p], wg_ss.at[h, k], wg_rs.at[h, k], dev)
            copy.start()
            wg_copies.append(copy)
        wg_r[h, my_p] = wg_s[h, my_p]

    def finish_grad(h):
        cols = slice(h * width, (h + 1) * width)
        back = finish_nets(gnet_copies, gnet_ref, h)
        y_ref[:, cols] = (dpre_ref[:, cols] + back * rs_ref[:, cols]).astype(BF16)

    for h in range(chunks - 1):
        finish_grad(h)

    for copy in wg_copies:
        copy.wait_recv()
    for h in range(chunks):
        piece = wg_r[h, 0].astype(F32)
        for p in range(1, plane):
            piece = piece + wg_r[h, p].astype(F32)
        wz_ref[my_l, :, h * width:(h + 1) * width] = piece.astype(wz_ref.dtype)
    wz_copies = []
    for k in range(1, loops):
        copy = remote(wz_ref.at[my_l], wz_ref.at[my_l], wz_ss.at[k], wz_rs.at[k],
                      {"loop": loop_peer(k)})
        copy.start()
        wz_copies.append(copy)
    finish_grad(chunks - 1)
    gf_copies = []
    for k in [*range(1, groups), 0]:
        peer = group_peer(k)
        w_rows = weight_ref[pl.ds(pl.multiple_of(peer * fw, fw), fw), :]
        gf_ref[k] = mm_nt(y_ref[...], w_rows).astype(BF16)
        if k > 0:
            copy = remote(gf_ref.at[k], gf_out.at[own_rows], gf_ss.at[k], gf_rs.at[k],
                          {"regroup": peer})
            copy.start()
            gf_copies.append(copy)
    gf_own = pltpu.make_async_copy(gf_ref.at[0], gf_out.at[own_rows], local_sem.at[1])
    gf_own.start()

    for copy in wz_copies:
        copy.wait_recv()
    piece = wz_ref[0].astype(F32)
    for l in range(1, loops):
        piece = piece + wz_ref[l].astype(F32)
    wf_ref[my_p] = piece.astype(wf_ref.dtype)
    wf_copies = []
    for k in range(1, plane):
        copy = remote(wf_ref.at[my_p], wf_ref.at[my_p], wf_ss.at[k], wf_rs.at[k],
                      plane_peer(k)[1])
        copy.start()
        wf_copies.append(copy)
    for copy in wf_copies:
        copy.wait_recv()
    wf_copy = pltpu.make_async_copy(wf_ref, wf_out, local_sem.at[0])
    wf_copy.start()
    out_copy.wait()
    gf_own.wait()
    wf_copy.wait()
    for copy in gf_copies:
        copy.wait_recv()
    for copies in (feat_copies, deg_copies, wg_copies, gf_copies, wz_copies, wf_copies,
                   *part_copies, *net_copies, *gpart_copies, *gnet_copies):
        for copy in copies:
            copy.wait_send()


def store_kernel(scale, out_in, gf_in, wf_in, out_hbm, gf_hbm, gw_hbm,
                 out_ref, gf_ref, wf_ref, gw_ref, sem):
    loads = [
        pltpu.make_async_copy(out_in, out_ref, sem.at[3]),
        pltpu.make_async_copy(gf_in, gf_ref, sem.at[4]),
        pltpu.make_async_copy(wf_in, wf_ref, sem.at[5]),
    ]
    stores = [
        pltpu.make_async_copy(out_ref, out_hbm, sem.at[0]),
        pltpu.make_async_copy(gf_ref, gf_hbm, sem.at[1]),
        pltpu.make_async_copy(gw_ref, gw_hbm, sem.at[2]),
    ]
    for load in loads:
        load.start()
    plane, rows_p, _ = wf_ref.shape
    for load, store in zip(loads, stores):
        load.wait()
        if store is stores[2]:
            for p in range(plane):
                gw_ref[p * rows_p:(p + 1) * rows_p, :] = wf_ref[p].astype(F32) * scale
        store.start()
    for store in stores:
        store.wait()


def per_device(groups, loops, replicas,
               features, weight, tiles, tile_row, tile_col, tile_width, cotangent):
    cells, chans = cotangent.shape[-2:]
    slots, edge = tiles.shape[-3:-1]
    total_rows, fw = features.shape[-2:]
    plane = groups * replicas
    rows_p = chans // plane
    chunks = chans // edge
    link = BF16 if rows_p % 16 == 0 else F32
    anym = pl.BlockSpec(memory_space=pl.ANY)
    dma = pltpu.SemaphoreType.DMA
    V = pltpu.VMEM
    scratch = [
        pltpu.SMEM((slots,), jnp.int32), pltpu.SMEM((slots,), jnp.int32),
        pltpu.SMEM((slots,), jnp.int32), V((chans, chans), BF16),
        V((slots, edge, edge), BF16), V((slots + 1, edge, edge), F32), V((edge, chans), BF16),
        V((groups, edge, fw), BF16), V((chans, edge), BF16), V((chans, chans), F32),
        V((cells, chans), BF16), V((groups, cells, fw), BF16),
        V((chans, cells), BF16), V((cells, 3 * edge), BF16), V((3 * edge, cells), BF16),
        V((cells, chans), F32), V((cells, chans), BF16), V((cells, chans), BF16),
        V((cells, chans), F32), V((cells, chans), F32),
        V((cells, chans), BF16), V((groups, cells, fw), BF16),
        V((3, edge, edge), BF16), V((2, edge, edge), BF16), V((edge, edge), F32),
        *([V((groups, 2, edge, fw), BF16)] * 2), V((chunks, 3, edge, edge), BF16),
        *([V((chunks, 2, edge, edge), BF16)] * 2), V((chunks, 3, edge, edge), BF16),
        *([V((chunks, plane, rows_p, edge), link)] * 2),
        V((loops, rows_p, chans), link), V((plane, rows_p, chans), link),
        dma((8,)), dma((groups,)), dma((groups,)), dma((2,)), dma((2,)),
        *([dma((groups, 2))] * 2), *([dma((chunks, 2))] * 6), dma((groups,)), dma((groups,)),
        *([dma((chunks, plane))] * 2), *([dma((loops,))] * 2), *([dma((plane,))] * 2),
    ]
    out, gf, wf = pl.pallas_call(
        functools.partial(layer_kernel, groups, loops, replicas),
        out_shape=(
            jax.ShapeDtypeStruct((cells, chans), BF16),
            jax.ShapeDtypeStruct((total_rows, fw), BF16),
            jax.ShapeDtypeStruct((plane, rows_p, chans), link),
        ),
        in_specs=[anym] * 7,
        out_specs=(anym, anym, anym),
        scratch_shapes=scratch,
        compiler_params=pltpu.CompilerParams(
            collective_id=0, has_side_effects=True, vmem_limit_bytes=60 << 20),
    )(tile_row[0, 0, 0], tile_col[0, 0, 0], tile_width[0, 0, 0], features[0, 0], weight,
      tiles[0, 0, 0], cotangent[0, 0, 0])
    out, gf, gw = pl.pallas_call(
        functools.partial(store_kernel, 1.0 / math.sqrt(cells * plane * loops)),
        out_shape=(
            jax.ShapeDtypeStruct((cells, chans), BF16),
            jax.ShapeDtypeStruct((total_rows, fw), BF16),
            jax.ShapeDtypeStruct((chans, chans), F32),
        ),
        in_specs=[anym] * 3,
        out_specs=(anym, anym, anym),
        scratch_shapes=[
            V((cells, chans), BF16), V((total_rows, fw), BF16), V((plane, rows_p, chans), link),
            V((chans, chans), F32), dma((6,)),
        ],
        compiler_params=pltpu.CompilerParams(vmem_limit_bytes=60 << 20),
    )(out, gf, wf)
    return out[None, None, None], gf[None, None], gw


def solution(mesh):
    sizes = dict(mesh.shape)
    return jax.shard_map(
        functools.partial(per_device, sizes["regroup"], sizes["loop"], sizes["replica"]),
        mesh=mesh,
        in_specs=(
            P("replica", "loop", None, "regroup"),
            P(),
            P("replica", "loop", "regroup", None, None, None),
            P("replica", "loop", "regroup", None),
            P("replica", "loop", "regroup", None),
            P("replica", "loop", "regroup", None),
            P("replica", "loop", "regroup", None, None),
        ),
        out_specs=(
            P("replica", "loop", "regroup", None, None),
            P("replica", "loop", None, "regroup"),
            P(),
        ),
        check_vma=False,
    )
```

```python
import functools
import math

import jax
import jax.numpy as jnp
from jax import lax
from jax.experimental import pallas as pl
from jax.experimental.pallas import tpu as pltpu
from jax.sharding import PartitionSpec as P

EPSILON = 1e-06
MESH = pl.DeviceIdType.MESH
F32 = jnp.float32
BF16 = jnp.bfloat16


def mm(a, b):
    return jnp.dot(a, b, preferred_element_type=F32)


def mm_nt(a, b):
    return lax.dot_general(a, b, (((1,), (1,)), ((), ())), preferred_element_type=F32)


def layer_kernel(
    groups, loops, replicas,
    row_hbm, col_hbm, width_hbm, feat_hbm, weight_hbm, tiles_hbm, cot_hbm,
    out_hbm, gf_out, wf_out,
    row_ref, col_ref, width_ref, weight_ref, tiles_ref, sums_ref, own_ref, usum_ref, ut_ref, direct_ref, cot_ref, x_ref, xt_ref, h_ref, ht_ref, rs_ref, y_ref, q_ref, acc_ref, dpre_ref,
    out_ref, gf_ref, deg_s, deg_r, deinv_ref, part_s, part_r, net_ref, gpart_s, gpart_r, gnet_ref,
    wg_s, wg_r, wz_ref, wf_ref,
    local_sem, feat_ss, feat_rs, deg_ss, deg_rs, part_ss, part_rs, net_ss, net_rs,
    gpart_ss, gpart_rs, gnet_ss, gnet_rs, gf_ss, gf_rs, wg_ss, wg_rs, wz_ss, wz_rs, wf_ss, wf_rs,
):
    slots, edge, _ = tiles_hbm.shape
    cells, chans = cot_hbm.shape
    fw = feat_hbm.shape[1]
    plane = groups * replicas
    width = edge
    chunks = chans // width
    my_g = lax.axis_index("regroup")
    my_l = lax.axis_index("loop")
    my_r = lax.axis_index("replica")
    my_p = my_r * groups + my_g

    def group_peer(k):
        return lax.rem(my_g + k, groups)

    def loop_peer(k):
        return lax.rem(my_l + k, loops)

    def plane_peer(k):
        peer = lax.rem(my_p + k, plane)
        return peer, {"replica": lax.div(peer, groups), "regroup": lax.rem(peer, groups)}

    prev_dev = {"loop": loop_peer(loops - 1)}
    next_dev = {"loop": loop_peer(1)}
    wraps_up = lax.div(my_l + 1, loops)
    ways = [
        (d, {"loop": loop_peer((1 - d) * (loops - 1) + d)}) for d in (wraps_up, 1 - wraps_up)
    ]

    def remote(src, dst, ss, rs, dev):
        return pltpu.make_async_remote_copy(
            src_ref=src, dst_ref=dst, send_sem=ss, recv_sem=rs, device_id=dev,
            device_id_type=MESH)

    barrier = pltpu.get_barrier_semaphore()
    for k in range(1, plane):
        pl.semaphore_signal(barrier, inc=1, device_id=plane_peer(k)[1], device_id_type=MESH)
    for k in range(1, loops):
        pl.semaphore_signal(barrier, inc=1, device_id={"loop": loop_peer(k)}, device_id_type=MESH)

    index_copies = [
        pltpu.make_async_copy(src, dst, local_sem.at[5 + i])
        for i, (src, dst) in enumerate(
            ((row_hbm, row_ref), (col_hbm, col_ref), (width_hbm, width_ref)))
    ]
    for copy in index_copies:
        copy.start()
    weight_copy = pltpu.make_async_copy(weight_hbm, weight_ref, local_sem.at[3])
    weight_copy.start()
    tiles_copy = pltpu.make_async_copy(tiles_hbm, tiles_ref, local_sem.at[0])
    tiles_copy.start()
    own_rows = pl.ds(pl.multiple_of(my_g * cells, cells), cells)
    own_copy = pltpu.make_async_copy(feat_hbm.at[own_rows], x_ref.at[my_g], local_sem.at[1])
    own_copy.start()
    cot_copy = pltpu.make_async_copy(cot_hbm, cot_ref, local_sem.at[2])
    cot_copy.start()

    pl.semaphore_wait(barrier, plane - 1 + loops - 1)

    feat_copies = []
    for k in range(1, groups):
        peer = group_peer(k)
        rows = pl.ds(pl.multiple_of(peer * cells, cells), cells)
        copy = remote(feat_hbm.at[rows], x_ref.at[my_g], feat_ss.at[k], feat_rs.at[k],
                      {"regroup": peer})
        copy.start()
        feat_copies.append(copy)

    for copy in index_copies:
        copy.wait()
    tiles_copy.wait()
    lane = lax.broadcasted_iota(jnp.int32, (1, edge), 1)
    blocks = cells // edge
    spots = 3 * blocks
    sums_ref[0] = jnp.zeros((edge, edge), F32)

    def add_tile(t, last):
        place = lax.rem(col_ref[t] - my_l + loops, loops)
        spot = row_ref[t] * 3 + jnp.where(place == 0, 1, jnp.where(place == 1, 2, 0))
        link = jnp.int32(0)
        for k in range(spots):
            link = jnp.where(spot == k, last[k], link)
        tile = jnp.where(lane < width_ref[t], tiles_ref[t].astype(F32), 0.0)
        sums_ref[t + 1] = tile + sums_ref[link]
        return tuple(jnp.where(spot == k, t + 1, last[k]) for k in range(spots))

    last = lax.fori_loop(0, slots, add_tile, (jnp.int32(0),) * spots, unroll=4)
    for b in range(blocks):
        for c in range(3):
            h_ref[b * edge:(b + 1) * edge, c * edge:(c + 1) * edge] = (
                sums_ref[last[b * 3 + c]].astype(BF16))
    for c in range(3):
        ht_ref[c * edge:(c + 1) * edge, :] = h_ref[:, c * edge:(c + 1) * edge].T

    deg_s[...] = mm(ht_ref[...], jnp.ones((cells, edge), BF16)).astype(BF16).reshape(3, edge, edge)
    deg_copies = [
        remote(deg_s.at[0], deg_r.at[1], deg_ss.at[0], deg_rs.at[1], prev_dev),
        remote(deg_s.at[2], deg_r.at[0], deg_ss.at[1], deg_rs.at[0], next_dev),
    ]
    for copy in deg_copies:
        copy.start()
    rs_ref[...] = lax.rsqrt(1.0 + mm(h_ref[...], jnp.ones((3 * edge, chans), BF16)))

    weight_copy.wait()
    own_copy.wait()

    def group_rows(k):
        source = lax.rem(my_g + groups - k, groups)
        return source, pl.ds(pl.multiple_of(source * fw, fw), fw)

    def send_sums(sums, send, recv, ss, rs):
        send[0] = sums[0:edge].astype(BF16)
        send[1] = sums[2 * edge:].astype(BF16)
        pair = [
            remote(send.at[d], recv.at[1 - d], ss.at[d], rs.at[1 - d], dev) for d, dev in ways
        ]
        for copy in pair:
            copy.start()
        return pair

    part_copies = []
    for k in range(groups):
        source, _ = group_rows(k)
        if k > 0:
            feat_copies[k - 1].wait_recv()
        xs = (x_ref[source].astype(F32) * rs_ref[:, 0:fw]).astype(BF16)
        sums = mm(ht_ref[...], xs)
        part_copies.append(send_sums(
            sums, part_s.at[k], part_r.at[k], part_ss.at[k], part_rs.at[k]))
        usum_ref[k] = sums[edge:2 * edge].astype(BF16)

    y32 = mm(x_ref[0], weight_ref[0:fw, :])
    for g in range(1, groups):
        y32 = y32 + mm(x_ref[g], weight_ref[g * fw:(g + 1) * fw, :])
    y_ref[...] = y32.astype(BF16)

    def send_nets(net, ss, rs):
        pair = [
            remote(net.at[1], net.at[2 - 2 * d], ss.at[d], rs.at[1 - d], dev) for d, dev in ways
        ]
        for copy in pair:
            copy.start()
        return pair

    def finish_nets(copies, net, h):
        for copy in copies[h]:
            copy.wait_recv()
        return mm(h_ref[...], net[h].reshape(3 * edge, width))

    for g in range(groups):
        xt_ref[g * fw:(g + 1) * fw, :] = x_ref[g].T
    for copy in deg_copies:
        copy.wait_recv()
    degree = (1.0 + deg_s[1].astype(F32) + deg_r[0].astype(F32) + deg_r[1].astype(F32))
    deinv_ref[...] = 1.0 / degree
    nets = None
    for k in range(groups):
        _, rows = group_rows(k)
        for copy in part_copies[k]:
            copy.wait_recv()
        total = (usum_ref[k].astype(F32) + part_r[k, 0].astype(F32) + part_r[k, 1].astype(F32)
                 ).astype(BF16)
        usum_ref[k] = total
        term = mm(total, weight_ref[rows, :])
        nets = term if nets is None else nets + term
    net_copies = []
    for h in range(chunks):
        net_ref[h, 1] = (nets[:, h * width:(h + 1) * width] * deinv_ref[...]).astype(BF16)
        net_copies.append(send_nets(net_ref.at[h], net_ss.at[h], net_rs.at[h]))
    for k in range(groups):
        _, rows = group_rows(k)
        ut_ref[rows, :] = usum_ref[k].T
    cot_copy.wait()
    for h in range(chunks):
        acc_ref[:, h * width:(h + 1) * width] = finish_nets(net_copies, net_ref, h)

    step = 64

    def middle(i, carry):
        rows = pl.ds(pl.multiple_of(i * step, step), step)
        root = rs_ref[rows, :]
        z = acc_ref[rows, :] * root
        inv = lax.rsqrt(jnp.mean(z * z, axis=-1, keepdims=True) + EPSILON)
        normed = z * inv
        pre = y_ref[rows, :].astype(F32) + normed
        sig = 1.0 / (1.0 + jnp.exp(-pre))
        out_ref[rows, :] = (pre * sig).astype(BF16)
        dpre = cot_ref[rows, :].astype(F32) * sig * (1.0 + pre * (1.0 - sig))
        dpre_ref[rows, :] = dpre
        dz = inv * (dpre - normed * jnp.mean(dpre * normed, axis=-1, keepdims=True))
        q_ref[rows, :] = (dz * root).astype(BF16)
        return carry

    lax.fori_loop(0, cells // step, middle, 0, unroll=True)
    out_copy = pltpu.make_async_copy(out_ref, out_hbm, local_sem.at[4])

    gpart_copies = []
    for h in range(chunks):
        cols = slice(h * width, (h + 1) * width)
        sums = mm(ht_ref[...], q_ref[:, cols])
        gpart_copies.append(send_sums(
            sums, gpart_s.at[h], gpart_r.at[h], gpart_ss.at[h], gpart_rs.at[h]))
        own_ref[:, cols] = sums[edge:2 * edge].astype(BF16)
    out_copy.start()

    rows_p = chans // plane
    direct_ref[...] = mm(xt_ref[...], dpre_ref[...].astype(BF16))
    gnet_copies, wg_copies = [], []
    for h in range(chunks):
        cols = slice(h * width, (h + 1) * width)
        for copy in gpart_copies[h]:
            copy.wait_recv()
        total = (own_ref[:, cols].astype(F32)
                 + gpart_r[h, 0].astype(F32) + gpart_r[h, 1].astype(F32))
        gnet_ref[h, 1] = (total * deinv_ref[...]).astype(BF16)
        gnet_copies.append(send_nets(gnet_ref.at[h], gnet_ss.at[h], gnet_rs.at[h]))
        wg = direct_ref[:, cols] + mm(ut_ref[...], gnet_ref[h, 1])
        for p in range(plane):
            wg_s[h, p] = wg[p * rows_p:(p + 1) * rows_p].astype(wg_s.dtype)
        for k in range(1, plane):
            peer, dev = plane_peer(k)
            copy = remote(wg_s.at[h, peer], wg_r.at[h, my_p], wg_ss.at[h, k], wg_rs.at[h, k], dev)
            copy.start()
            wg_copies.append(copy)
        wg_r[h, my_p] = wg_s[h, my_p]

    def finish_grad(h):
        cols = slice(h * width, (h + 1) * width)
        back = finish_nets(gnet_copies, gnet_ref, h)
        y_ref[:, cols] = (dpre_ref[:, cols] + back * rs_ref[:, cols]).astype(BF16)

    for h in range(chunks - 1):
        finish_grad(h)

    for copy in wg_copies:
        copy.wait_recv()
    for h in range(chunks):
        piece = wg_r[h, 0].astype(F32)
        for p in range(1, plane):
            piece = piece + wg_r[h, p].astype(F32)
        wz_ref[my_l, :, h * width:(h + 1) * width] = piece.astype(wz_ref.dtype)
    wz_copies = []
    for k in range(1, loops):
        copy = remote(wz_ref.at[my_l], wz_ref.at[my_l], wz_ss.at[k], wz_rs.at[k],
                      {"loop": loop_peer(k)})
        copy.start()
        wz_copies.append(copy)
    finish_grad(chunks - 1)
    gf_copies = []
    for k in [*range(1, groups), 0]:
        peer = group_peer(k)
        w_rows = weight_ref[pl.ds(pl.multiple_of(peer * fw, fw), fw), :]
        gf_ref[k] = mm_nt(y_ref[...], w_rows).astype(BF16)
        if k > 0:
            copy = remote(gf_ref.at[k], gf_out.at[own_rows], gf_ss.at[k], gf_rs.at[k],
                          {"regroup": peer})
            copy.start()
            gf_copies.append(copy)
    gf_own = pltpu.make_async_copy(gf_ref.at[0], gf_out.at[own_rows], local_sem.at[1])
    gf_own.start()

    for copy in wz_copies:
        copy.wait_recv()
    piece = wz_ref[0].astype(F32)
    for l in range(1, loops):
        piece = piece + wz_ref[l].astype(F32)
    wf_ref[my_p] = piece.astype(wf_ref.dtype)
    wf_copies = []
    for k in range(1, plane):
        copy = remote(wf_ref.at[my_p], wf_ref.at[my_p], wf_ss.at[k], wf_rs.at[k],
                      plane_peer(k)[1])
        copy.start()
        wf_copies.append(copy)
    for copy in wf_copies:
        copy.wait_recv()
    wf_copy = pltpu.make_async_copy(wf_ref, wf_out, local_sem.at[0])
    wf_copy.start()
    out_copy.wait()
    gf_own.wait()
    wf_copy.wait()
    for copy in gf_copies:
        copy.wait_recv()
    for copies in (feat_copies, deg_copies, wg_copies, gf_copies, wz_copies, wf_copies,
                   *part_copies, *net_copies, *gpart_copies, *gnet_copies):
        for copy in copies:
            copy.wait_send()


def store_kernel(scale, out_in, gf_in, wf_in, out_hbm, gf_hbm, gw_hbm,
                 out_ref, gf_ref, wf_ref, gw_ref, sem):
    loads = [
        pltpu.make_async_copy(out_in, out_ref, sem.at[3]),
        pltpu.make_async_copy(gf_in, gf_ref, sem.at[4]),
        pltpu.make_async_copy(wf_in, wf_ref, sem.at[5]),
    ]
    stores = [
        pltpu.make_async_copy(out_ref, out_hbm, sem.at[0]),
        pltpu.make_async_copy(gf_ref, gf_hbm, sem.at[1]),
        pltpu.make_async_copy(gw_ref, gw_hbm, sem.at[2]),
    ]
    for load in loads:
        load.start()
    plane, rows_p, _ = wf_ref.shape
    for load, store in zip(loads, stores):
        load.wait()
        if store is stores[2]:
            for p in range(plane):
                gw_ref[p * rows_p:(p + 1) * rows_p, :] = wf_ref[p].astype(F32) * scale
        store.start()
    for store in stores:
        store.wait()


def per_device(groups, loops, replicas,
               features, weight, tiles, tile_row, tile_col, tile_width, cotangent):
    cells, chans = cotangent.shape[-2:]
    slots, edge = tiles.shape[-3:-1]
    total_rows, fw = features.shape[-2:]
    plane = groups * replicas
    rows_p = chans // plane
    chunks = chans // edge
    link = BF16 if rows_p % 16 == 0 else F32
    anym = pl.BlockSpec(memory_space=pl.ANY)
    dma = pltpu.SemaphoreType.DMA
    V = pltpu.VMEM
    scratch = [
        pltpu.SMEM((slots,), jnp.int32), pltpu.SMEM((slots,), jnp.int32),
        pltpu.SMEM((slots,), jnp.int32), V((chans, chans), BF16),
        V((slots, edge, edge), BF16), V((slots + 1, edge, edge), F32), V((edge, chans), BF16),
        V((groups, edge, fw), BF16), V((chans, edge), BF16), V((chans, chans), F32),
        V((cells, chans), BF16), V((groups, cells, fw), BF16),
        V((chans, cells), BF16), V((cells, 3 * edge), BF16), V((3 * edge, cells), BF16),
        V((cells, chans), F32), V((cells, chans), BF16), V((cells, chans), BF16),
        V((cells, chans), F32), V((cells, chans), F32),
        V((cells, chans), BF16), V((groups, cells, fw), BF16),
        V((3, edge, edge), BF16), V((2, edge, edge), BF16), V((edge, edge), F32),
        *([V((groups, 2, edge, fw), BF16)] * 2), V((chunks, 3, edge, edge), BF16),
        *([V((chunks, 2, edge, edge), BF16)] * 2), V((chunks, 3, edge, edge), BF16),
        *([V((chunks, plane, rows_p, edge), link)] * 2),
        V((loops, rows_p, chans), link), V((plane, rows_p, chans), link),
        dma((8,)), dma((groups,)), dma((groups,)), dma((2,)), dma((2,)),
        *([dma((groups, 2))] * 2), *([dma((chunks, 2))] * 6), dma((groups,)), dma((groups,)),
        *([dma((chunks, plane))] * 2), *([dma((loops,))] * 2), *([dma((plane,))] * 2),
    ]
    out, gf, wf = pl.pallas_call(
        functools.partial(layer_kernel, groups, loops, replicas),
        out_shape=(
            jax.ShapeDtypeStruct((cells, chans), BF16),
            jax.ShapeDtypeStruct((total_rows, fw), BF16),
            jax.ShapeDtypeStruct((plane, rows_p, chans), link),
        ),
        in_specs=[anym] * 7,
        out_specs=(anym, anym, anym),
        scratch_shapes=scratch,
        compiler_params=pltpu.CompilerParams(
            collective_id=0, has_side_effects=True, vmem_limit_bytes=60 << 20),
    )(tile_row[0, 0, 0], tile_col[0, 0, 0], tile_width[0, 0, 0], features[0, 0], weight,
      tiles[0, 0, 0], cotangent[0, 0, 0])
    out, gf, gw = pl.pallas_call(
        functools.partial(store_kernel, 1.0 / math.sqrt(cells * plane * loops)),
        out_shape=(
            jax.ShapeDtypeStruct((cells, chans), BF16),
            jax.ShapeDtypeStruct((total_rows, fw), BF16),
            jax.ShapeDtypeStruct((chans, chans), F32),
        ),
        in_specs=[anym] * 3,
        out_specs=(anym, anym, anym),
        scratch_shapes=[
            V((cells, chans), BF16), V((total_rows, fw), BF16), V((plane, rows_p, chans), link),
            V((chans, chans), F32), dma((6,)),
        ],
        compiler_params=pltpu.CompilerParams(vmem_limit_bytes=60 << 20),
    )(out, gf, wf)
    return out[None, None, None], gf[None, None], gw


def solution(mesh):
    sizes = dict(mesh.shape)
    return jax.shard_map(
        functools.partial(per_device, sizes["regroup"], sizes["loop"], sizes["replica"]),
        mesh=mesh,
        in_specs=(
            P("replica", "loop", None, "regroup"),
            P(),
            P("replica", "loop", "regroup", None, None, None),
            P("replica", "loop", "regroup", None),
            P("replica", "loop", "regroup", None),
            P("replica", "loop", "regroup", None),
            P("replica", "loop", "regroup", None, None),
        ),
        out_specs=(
            P("replica", "loop", "regroup", None, None),
            P("replica", "loop", None, "regroup"),
            P(),
        ),
        check_vma=False,
    )
```
